128 devices in a mesh: gx: 2 (over core), gy: 16 (over y, x), gz: 4 (over z).
Axes of the slice: x: 4, y: 4, z: 4, core: 2. Of those that a mesh axis runs over, the one named last changes fastest.
Arguments:
- places: float32 [3, 12, 16, 24, 128], P(None, 'gx', 'gy', 'gz'), may hold values from 0.45 to 8.35, as said below
- velocity: float32 [3, 12, 16, 24, 128], P(None, 'gx', 'gy', 'gz'), may hold values from -6 to 6
- forces_old: float32 [3, 12, 16, 24, 128], P(None, 'gx', 'gy', 'gz'), may hold values from -48 to 48
- counts: int32 [12, 16, 24], P('gx', 'gy', 'gz'), may hold values from 16 to 120, as said below
- mig_atom: int32 [2, 16, 4, 16], P('gx', 'gy', 'gz'), may hold values from 0 to 4607, as said below
- mig_face: int32 [2, 16, 4, 16], P('gx', 'gy', 'gz'), may hold values from 0 to 5, as said below
Outputs:
- new_places: float32 [3, 12, 16, 24, 128], P(None, 'gx', 'gy', 'gz')
- new_velocity: float32 [3, 12, 16, 24, 128], P(None, 'gx', 'gy', 'gz')
- new_forces: float32 [3, 12, 16, 24, 128], P(None, 'gx', 'gy', 'gz')
The draws below stay inside these ranges and needn't reach their ends.
Inputs may be any that keep to these rules, and one draw needn't show every extreme that they name: `places`: within a cell and between neighbouring cells, any two slots lie at least 0.7 apart. `counts`: some cell holds exactly 120 atoms. `mig_atom`: each device's 16 entries name occupied slots of 16 distinct cells. `mig_face`: each entry's cell lies on the named face of its device's block.
All inputs are finite; a program needn't handle non-finite values.
Results may differ from the reference program's by a relative error of at most 0.0003.
Values sent between devices are 32-bit elements; how exact they have to be, the bound alone decides.
A program may use at most 64 MiB of HBM per device.

```python
import math
import jax
import jax.numpy as jnp
from jax import lax

CAP = 128
MIG = 16
NX = 12
NY = 16
NZ = 24
N_GX = 2
N_GY = 16
N_GZ = 4


def draw_count_table(key):
    base_key = jax.random.fold_in(key, 11)
    low_count = CAP // 8
    high_count = CAP - 8
    spread = high_count - low_count
    first_draw = jax.random.randint(jax.random.fold_in(base_key, 1), (NX, NY, NZ), 0, spread + 1)
    second = jax.random.randint(jax.random.fold_in(base_key, 2), (NX, NY, NZ), 0, spread + 1)
    count_table = low_count + first_draw * second // spread
    cell_total = NX * NY * NZ
    chosen = jax.random.randint(jax.random.fold_in(base_key, 3), (), 0, cell_total)
    flat_table = jnp.where(jnp.arange(cell_total) == chosen, high_count, count_table.reshape(-1))
    return flat_table.reshape(NX, NY, NZ).astype(jnp.int32)


def draw_moves(key):
    count_table = draw_count_table(key)
    base_key = jax.random.fold_in(key, 23)
    local_x = NX // N_GX
    local_y = NY // N_GY
    local_z = NZ // N_GZ
    cell_count = local_x * local_y * local_z
    device_total = N_GX * N_GY * N_GZ
    cell_index = jnp.arange(cell_count)
    pos_x = cell_index // (local_y * local_z)
    pos_y = cell_index // local_z % local_y
    pos_z = cell_index % local_z
    border = (pos_x == 0) | (pos_x == local_x - 1) | (pos_y == 0) | (pos_y == local_y - 1) | (pos_z == 0) | (pos_z == local_z - 1)
    scores = jax.random.randint(jax.random.fold_in(base_key, 1), (device_total, cell_count), 0, 1 << 14)
    keyed_scores = jnp.where(border[None, :], scores, 1 << 14) * cell_count + cell_index[None, :]
    picked = jnp.argsort(keyed_scores, axis=1)[:, :MIG]
    pick_x = picked // (local_y * local_z)
    pick_y = picked // local_z % local_y
    pick_z = picked % local_z
    on_face = jnp.stack([pick_x == 0, pick_x == local_x - 1, pick_y == 0, pick_y == local_y - 1, pick_z == 0, pick_z == local_z - 1], axis=-1)
    face_scores = jax.random.randint(jax.random.fold_in(base_key, 2), (device_total, MIG, 6), 0, 1 << 10) * 8 + jnp.arange(6)
    face_pick = jnp.argmax(jnp.where(on_face, face_scores, -1), axis=-1).astype(jnp.int32)
    device_index = jnp.arange(device_total)[:, None]
    dev_x = device_index // (N_GY * N_GZ)
    dev_y = device_index // N_GZ % N_GY
    dev_z = device_index % N_GZ
    held = count_table[dev_x * local_x + pick_x, dev_y * local_y + pick_y, dev_z * local_z + pick_z]
    slot_pick = jax.random.randint(jax.random.fold_in(base_key, 3), (device_total, MIG), 0, held)
    atom_pick = (picked * CAP + slot_pick).astype(jnp.int32)
    return (atom_pick.reshape(N_GX, N_GY, N_GZ, MIG), face_pick.reshape(N_GX, N_GY, N_GZ, MIG))


def draw_counts(key, part):
    return draw_count_table(key)


def draw_mig_atom(key, part):
    return draw_moves(key)[0]


def draw_mig_face(key, part):
    return draw_moves(key)[1]


def draw_places(key, part):
    order_key = jax.random.fold_in(key, 31)
    jitter_key = jax.random.fold_in(key, 37)
    scores = jax.random.randint(order_key, (NX, NY, NZ, CAP), 0, 1 << 16) * CAP + jnp.arange(CAP)
    site_index = jnp.argsort(scores, axis=-1)
    lattice = jnp.stack([site_index % 4, site_index // 4 % 4, site_index // 16]).astype(jnp.float32) * 1.1 + 0.55
    wobble = jnp.clip(0.03 * jax.random.normal(jitter_key, (3, NX, NY, NZ, CAP), jnp.float32), -0.06, 0.06)
    return lattice + wobble


def steps_of(stream_key, extent, pieces, smallest, top_value):
    def one(dim, parts):
        steps = jax.random.uniform(jax.random.fold_in(jax.random.fold_in(stream_key, 6), dim), (parts,), jnp.float32, smallest / len(pieces), top_value / len(pieces))
        return jnp.repeat(jnp.exp(steps), extent[dim] // parts).reshape((-1,) + (1,) * (len(extent) - dim - 1))

    gain = one(*pieces[0])
    for cut in pieces[1:]:
        gain = gain * one(*cut)
    return gain


def normal_values(rng, shape, scale, bound, pieces=(), kind=jnp.bfloat16):
    gain = steps_of(rng, shape, pieces, -0.22, 0.18) if pieces else 1.0
    values = jax.random.normal(rng, shape, jnp.float32) * scale * gain
    return jnp.minimum(jnp.maximum(values, -bound), bound).astype(kind)


def setup_inputs(seed: int = 0) -> dict:
    key_of = jax.random.split(jax.random.key(seed), 7)
    return {
        "places": draw_places(jax.random.fold_in(key_of[6], 71), 0),
        "velocity": normal_values(key_of[1], (3, NX, NY, NZ, CAP), 1.0, 6.0, ((1, 2), (2, 16), (3, 4)), jnp.float32),
        "forces_old": normal_values(key_of[2], (3, NX, NY, NZ, CAP), 8.0, 48.0, ((1, 2), (2, 16), (3, 4)), jnp.float32),
        "counts": draw_counts(jax.random.fold_in(key_of[6], 71), 0),
        "mig_atom": draw_mig_atom(jax.random.fold_in(key_of[6], 71), 0),
        "mig_face": draw_mig_face(jax.random.fold_in(key_of[6], 71), 0),
    }


step_size = 0.005
cut_radius = 2.5
spacing = 1.1
edge_force = 24.0 * (2.0 * cut_radius ** (-13) - cut_radius ** (-7))

def cell_sides(slot_count):
    return (4.0 * spacing, 4.0 * spacing, spacing * (slot_count // 16))

def half_offsets():
    chosen = []
    for step_z in (-1, 0, 1):
        for step_y in (-1, 0, 1):
            for step_x in (-1, 0, 1):
                if step_z > 0 or (step_z == 0 and (step_y > 0 or (step_y == 0 and step_x >= 0))):
                    chosen.append((step_x, step_y, step_z))
    return chosen

def pair_terms(own_places, other_places, own_alive, other_alive, offset_vec, same_cell):
    shaped = jnp.asarray(offset_vec, own_places.dtype).reshape((3,) + (1,) * own_places.ndim)
    delta_vec = own_places[..., :, None] - (other_places[..., None, :] + shaped)
    distance = lax.optimization_barrier(jnp.sum(delta_vec * delta_vec, axis=0))
    weight = own_alive[..., :, None] * other_alive[..., None, :]
    if same_cell:
        slot_count = own_places.shape[-1]
        rows_iota = lax.broadcasted_iota(jnp.int32, (slot_count, slot_count), 0)
        cols_iota = lax.broadcasted_iota(jnp.int32, (slot_count, slot_count), 1)
        weight = weight * (rows_iota != cols_iota).astype(weight.dtype)
    inside = jnp.where(distance < cut_radius * cut_radius, weight, jnp.zeros_like(weight))
    safe_sq = jnp.where(inside > 0.0, distance, jnp.ones_like(distance))
    inverse = 1.0 / safe_sq
    sixth_power = inverse * inverse * inverse
    magnitude = (24.0 * inverse * sixth_power * (2.0 * sixth_power - 1.0) - edge_force * lax.rsqrt(safe_sq)) * inside
    pulled = delta_vec * magnitude
    return (lax.optimization_barrier(jnp.sum(pulled, axis=-1)), -lax.optimization_barrier(jnp.sum(pulled, axis=-2)))

def split_blocks(array, block_depth):
    lead, size_x, size_y, size_z, slot_count = array.shape
    shaped = array.reshape(lead, size_x, size_y, size_z // block_depth, block_depth, slot_count)
    return shaped.transpose(3, 0, 1, 2, 4, 5)

def join_blocks(array):
    block_total, lead, size_x, size_y, block_depth, slot_count = array.shape
    return array.transpose(1, 2, 3, 0, 4, 5).reshape(lead, size_x, size_y, block_total * block_depth, slot_count)

def all_forces(places, alive_mask):
    full_state = jnp.concatenate([places, alive_mask[None]], axis=0)
    block_depth = math.gcd(places.shape[3], 2)
    cell_side = cell_sides(places.shape[4])
    total_force = jnp.zeros_like(places)
    own_blocks = split_blocks(full_state, block_depth)
    for step_x, step_y, step_z in half_offsets():
        rolled = jnp.roll(full_state, (-step_x, -step_y, -step_z), axis=(1, 2, 3))
        same_cell = (step_x, step_y, step_z) == (0, 0, 0)
        offset_vec = (step_x * cell_side[0], step_y * cell_side[1], step_z * cell_side[2])

        def one_block(pair_blocks):
            own_block, side_block = pair_blocks
            return pair_terms(own_block[:3], side_block[:3], own_block[3], side_block[3], offset_vec, same_cell)
        near_term, far_term = lax.map(one_block, (own_blocks, split_blocks(rolled, block_depth)))
        total_force = total_force + join_blocks(near_term)
        if not same_cell:
            total_force = total_force + jnp.roll(join_blocks(far_term), (step_x, step_y, step_z), axis=(1, 2, 3))
    return total_force

def reference(places, velocity, forces_old, counts, mig_atom, mig_face):
    size_x, size_y, size_z, slot_count = places.shape[1:]
    side_x, side_y, side_z = cell_sides(slot_count)
    alive_mask = (lax.broadcasted_iota(jnp.int32, places.shape[1:], 3) < counts[..., None]).astype(places.dtype)
    half_velocity = velocity + 0.5 * step_size * forces_old
    drifted = places + step_size * half_velocity
    local_x = size_x // N_GX
    local_y = size_y // N_GY
    local_z = size_z // N_GZ
    grid_shape = mig_atom.shape
    dev_x = lax.broadcasted_iota(jnp.int32, grid_shape, 0)
    dev_y = lax.broadcasted_iota(jnp.int32, grid_shape, 1)
    dev_z = lax.broadcasted_iota(jnp.int32, grid_shape, 2)
    cell_id = mig_atom // slot_count
    slot_id = mig_atom % slot_count
    glob_x = dev_x * local_x + cell_id // (local_y * local_z)
    glob_y = dev_y * local_y + cell_id // local_z % local_y
    glob_z = dev_z * local_z + cell_id % local_z
    source = (((glob_x * size_y + glob_y) * size_z + glob_z) * slot_count + slot_id).reshape(-1)
    face_axis = mig_face // 2
    face_sign = 2 * (mig_face % 2) - 1
    dest_x = (glob_x + face_sign * (face_axis == 0).astype(jnp.int32)) % size_x
    dest_y = (glob_y + face_sign * (face_axis == 1).astype(jnp.int32)) % size_y
    dest_z = (glob_z + face_sign * (face_axis == 2).astype(jnp.int32)) % size_z
    dest_cell = ((dest_x * size_y + dest_y) * size_z + dest_z).reshape(-1)
    order_key = (mig_face + 1 - 2 * (mig_face % 2)).reshape(-1)
    flat_sign = face_sign.reshape(-1).astype(places.dtype)
    flat_axis = face_axis.reshape(-1)
    flat_places = drifted.reshape(3, -1)
    flat_velocity = half_velocity.reshape(3, -1)
    flat_alive = alive_mask.reshape(-1)
    along_axis = (lax.broadcasted_iota(jnp.int32, (3, flat_axis.shape[0]), 0) == flat_axis[None, :]).astype(places.dtype)
    side_vec = jnp.asarray((side_x, side_y, side_z), places.dtype)[:, None]
    carried = flat_places[:, source] - along_axis * flat_sign[None, :] * side_vec
    carried_velocity = flat_velocity[:, source]
    flat_alive = flat_alive.at[source].set(0.0)
    cell_total = size_x * size_y * size_z
    arrival_rank = jnp.zeros_like(dest_cell)
    for face_index in range(6):
        hit_count = jnp.zeros((cell_total,), jnp.int32).at[dest_cell].add((order_key == face_index).astype(jnp.int32))
        arrival_rank = arrival_rank + jnp.where(order_key > face_index, hit_count[dest_cell], 0)
    target = dest_cell * slot_count + counts.reshape(-1)[dest_cell] + arrival_rank
    flat_places = flat_places.at[:, target].set(carried)
    flat_velocity = flat_velocity.at[:, target].set(carried_velocity)
    flat_alive = flat_alive.at[target].set(1.0)
    settled_places = flat_places.reshape(places.shape)
    settled_velocity = flat_velocity.reshape(places.shape)
    settled_alive = flat_alive.reshape(alive_mask.shape)
    new_forces = all_forces(settled_places, settled_alive) * settled_alive[None]
    new_velocity = (settled_velocity + 0.5 * step_size * new_forces) * settled_alive[None]
    new_places = settled_places * settled_alive[None]
    return (new_places, new_velocity, new_forces)
```

```python
import functools

import jax
import jax.numpy as jnp
from jax import lax
from jax.experimental import pallas as pl
from jax.experimental.pallas import tpu as pltpu
from jax.sharding import PartitionSpec as P

MESH = pl.DeviceIdType.MESH
F32 = jnp.float32
I32 = jnp.int32
STEP = 0.005
RC = 2.5
SPACING = 1.1
EDGE = 24.0 * (2.0 * RC ** (-13) - RC ** (-7))
SIDE = (4.0 * SPACING, 4.0 * SPACING, SPACING * 8)
FAR = 1.0e4
REACH = RC * 1.0005
SX, SZ, CAP, MIG = 6, 6, 128, 16
NDIR = 27
ROWS = 4
NL = 2
NT = 32


def iota(shape, dim):
    return lax.broadcasted_iota(I32, shape, dim)


def exchange_kernel(sizes, counts, atoms, faces, places, velocity, forces,
                    own, vel, yblk, slab, zrow,
                    drift, half, letter, inbox, zsend,
                    lsend, lrecv, bsend, brecv, ssend, srecv, zs, zr):
    n_gx, n_gy, n_gz = sizes
    me = (lax.axis_index("gx"), lax.axis_index("gy"), lax.axis_index("gz"))

    def at(dx, dy, dz):
        return (
            lax.rem(me[0] + dx + n_gx, n_gx),
            lax.rem(me[1] + dy + n_gy, n_gy),
            lax.rem(me[2] + dz + n_gz, n_gz),
        )

    barrier = pltpu.get_barrier_semaphore()
    around = [
        (dx, dy, dz) for dx in (0, 1) for dy in (-1, 0, 1) for dz in (-1, 0, 1) if (dx, dy, dz) != (0, 0, 0)
    ]
    for step in around:
        pl.semaphore_signal(barrier, inc=1, device_id=at(*step), device_id_type=MESH)

    for c in range(3):
        for x in range(SX):
            h = velocity[c, x] + 0.5 * STEP * forces[c, x]
            half[c, x] = h
            drift[c, x] = places[c, x] + STEP * h

    sub8 = iota((8, CAP), 0)
    lane8 = iota((8, CAP), 1)
    lane1 = iota((1, CAP), 1)
    out_letter = jnp.where(sub8 == 6, -1.0, 0.0).astype(F32)
    leaving_cell = jnp.full((1, CAP), -1.0, F32)
    leaving_slot = jnp.full((1, CAP), -1.0, F32)
    for k in range(MIG):
        atom = atoms[0, 0, 0, k]
        face = faces[0, 0, 0, k]
        cell = lax.shift_right_logical(atom, 7)
        slot = atom & 127
        cx = lax.div(cell, SZ)
        cz = lax.rem(cell, SZ)
        axis = lax.shift_right_logical(face, 1)
        up = face & 1
        tile = jnp.zeros((8, CAP), F32)
        for c in range(6):
            source = drift if c < 3 else half
            row = source[c % 3, cx, pl.ds(cz, 1), :]
            tile = jnp.where(sub8 == c, jnp.broadcast_to(row, (8, CAP)), tile)
        column = jnp.sum(jnp.where(lane8 == slot, tile, 0.0), axis=1, keepdims=True)
        sign = (2 * up - 1).astype(F32)
        shift = jnp.where(axis == 2, SIDE[2], SIDE[0]).astype(F32) * sign
        sub_col = iota((8, 1), 0)
        column = column - jnp.where(sub_col == axis, shift, 0.0)
        nx = jnp.where(axis == 0, (1 - up) * (SX - 1), cx)
        nz = jnp.where(axis == 2, (1 - up) * (SZ - 1), cz)
        column = jnp.where(sub_col == 6, (nx * 8 + nz).astype(F32), column)
        out_letter = jnp.where(lane8 == 16 * (face ^ 1) + k, column, out_letter)
        leaving_cell = jnp.where(lane1 == 96 + k, (cx * 8 + cz).astype(F32), leaving_cell)
        leaving_slot = jnp.where(lane1 == 96 + k, slot.astype(F32), leaving_slot)
    letter[...] = out_letter

    pl.semaphore_wait(barrier, len(around))

    posts = []
    for box, step in enumerate(((1, 0, 0), (0, 1, 0), (0, -1, 0), (0, 0, 1), (0, 0, -1))):
        post = pltpu.make_async_remote_copy(
            src_ref=letter, dst_ref=inbox.at[box], send_sem=lsend.at[box], recv_sem=lrecv.at[box],
            device_id=at(*step), device_id_type=MESH,
        )
        post.start()
        posts.append(post)

    count_rows = []
    for x in range(SX):
        row = jnp.zeros((8, CAP), I32)
        for z in range(SZ):
            row = jnp.where(sub8 == z, counts[x, 0, z], row)
        count_rows.append(row)

    for post in posts:
        post.wait_recv()
    got = inbox[4]
    for box, top in ((3, 80), (2, 64), (1, 48), (0, 32)):
        got = jnp.where(lane8 < top, inbox[box], got)
    arriving_cell = jnp.where(lane1 < 96, got[6:7, :], -1.0)
    sub8f = sub8.astype(F32)
    here = []
    gone = []
    for x in range(SX):
        here.append((jnp.broadcast_to(arriving_cell, (8, CAP)) == sub8f + 8.0 * x).astype(F32))
        gone.append((jnp.broadcast_to(leaving_cell, (8, CAP)) == sub8f + 8.0 * x).astype(F32))
    here_all = jnp.concatenate(here, axis=0)
    gone_all = jnp.concatenate(gone, axis=0)
    earlier = (iota((CAP, CAP), 0) < iota((CAP, CAP), 1)).astype(jnp.bfloat16)
    rank = jnp.dot(here_all.astype(jnp.bfloat16), earlier, preferred_element_type=F32)
    slot_table = here_all * (rank + jnp.concatenate(count_rows, axis=0).astype(F32))
    target = jnp.sum(slot_table, axis=0, keepdims=True)
    target = jnp.where(lane1 < 96, target, leaving_slot)
    slot_hit = (jnp.broadcast_to(target, (CAP, CAP)) == iota((CAP, CAP), 0).astype(F32)).astype(jnp.bfloat16)
    pieces = [(here_all - gone_all).astype(jnp.bfloat16)]
    for c in range(6):
        part = here_all * jnp.broadcast_to(jnp.where(lane1 < 96, got[c : c + 1, :], 0.0), here_all.shape)
        for _ in range(3):
            top = part.astype(jnp.bfloat16)
            pieces.append(top)
            part = part - top.astype(F32)
    landed = lax.dot_general(
        jnp.concatenate(pieces, axis=0), slot_hit, (((1,), (1,)), ((), ())), preferred_element_type=F32
    )
    n = SX * 8

    def arrived(c, x):
        base = n * (1 + 3 * c) + 8 * x
        return (
            landed[base : base + SZ] + landed[base + n : base + n + SZ] + landed[base + 2 * n : base + 2 * n + SZ]
        )

    lane6 = iota((SZ, CAP), 1)
    for x in range(SX):
        delta = landed[8 * x : 8 * x + SZ]
        live = (lane6 < count_rows[x][:SZ]).astype(F32) + delta > 0.5
        came = delta > 0.5
        for c in range(3):
            place = jnp.where(came, arrived(c, x), drift[c, x])
            place = jnp.where(live, place, FAR)
            own[c, x, 0:SZ] = place
            own[c, x, SZ:8] = jnp.full((8 - SZ, CAP), FAR, F32)
            zsend[0, c, x : x + 1] = place[0:1]
            zsend[1, c, x : x + 1] = place[SZ - 1 : SZ]
            speed = jnp.where(came, arrived(3 + c, x), half[c, x])
            vel[c, x] = jnp.where(live, speed, 0.0)
    for side in range(2):
        for c in range(3):
            zsend[side, c, SX:8] = jnp.full((8 - SX, CAP), FAR, F32)

    copies = []

    def send(src, dst, ssem, rsem, step):
        copy = pltpu.make_async_remote_copy(
            src_ref=src, dst_ref=dst, send_sem=ssem, recv_sem=rsem, device_id=at(*step), device_id_type=MESH
        )
        copy.start()
        copies.append(copy)

    for i, dy in enumerate((1, -1)):
        send(own, yblk.at[i], bsend.at[i], brecv.at[i], (0, dy, 0))
    for dy in (1, -1, 0):
        there = 1 - dy
        for s, x in ((0, 0), (1, SX - 1)):
            send(own.at[:, x], slab.at[there, s], ssend.at[there, s], srecv.at[there, s], (1, dy, 0))
    for dy in (1, -1, 0):
        there = 1 - dy
        for dx in (0, 1):
            for zi, dz in ((0, -1), (1, 1)):
                send(zsend.at[zi], zrow.at[there, dx, 1 - zi], zs.at[there, dx, zi], zr.at[there, dx, 1 - zi], (dx, dy, dz))
    for post in posts:
        post.wait_send()
    for copy in copies:
        copy.wait_send()
    for i, dy in enumerate((1, -1)):
        pltpu.make_async_remote_copy(
            src_ref=own, dst_ref=yblk.at[i], send_sem=bsend.at[i], recv_sem=brecv.at[i],
            device_id=at(0, dy, 0), device_id_type=MESH).wait_recv()
    for y in range(3):
        for s in range(2):
            pltpu.make_async_remote_copy(
                src_ref=own.at[:, 0], dst_ref=slab.at[y, s], send_sem=ssend.at[y, s], recv_sem=srecv.at[y, s],
                device_id=at(1, 0, 0), device_id_type=MESH).wait_recv()
        for g in range(2):
            for s in range(2):
                pltpu.make_async_remote_copy(
                    src_ref=zsend.at[0], dst_ref=zrow.at[y, g, s], send_sem=zs.at[y, g, s], recv_sem=zr.at[y, g, s],
                    device_id=at(0, 0, 1), device_id_type=MESH).wait_recv()


def force_kernel(own, vel, yblk, slab, zrow, out_places, out_velocity, out_forces,
                 near, packed, lists, columns, force_columns, totals):
    sub8 = iota((8, CAP), 0)
    lane8 = iota((8, CAP), 1)

    for y in range(3):
        for c in range(3):
            for xi in range(8):
                if xi == 0:
                    tile = slab[y, 1, c]
                    low, high = (zrow[y, 1, s, c, SX - 1 : SX] for s in (0, 1))
                elif xi == 7:
                    tile = slab[y, 0, c]
                    low, high = (zrow[y, 1, s, c, 0:1] for s in (0, 1))
                else:
                    tile = own[c, xi - 1] if y == 1 else yblk[y // 2, c, xi - 1]
                    low, high = (zrow[y, 0, s, c, xi - 1 : xi] for s in (0, 1))
                below = jnp.where(sub8 == 0, jnp.broadcast_to(low, (8, CAP)), pltpu.roll(tile, 1, 0))
                above = jnp.where(sub8 == SZ - 1, jnp.broadcast_to(high, (8, CAP)), pltpu.roll(tile, 7, 0))
                for zi, value in enumerate((below, tile, above)):
                    if c == 1 and y != 1:
                        value = value + (y - 1) * SIDE[1]
                    if c == 2 and zi != 1:
                        value = value + (zi - 1) * SIDE[2]
                    near[zi, c, y, xi] = value

    prefix = (iota((CAP, CAP), 0) <= iota((CAP, CAP), 1)).astype(jnp.bfloat16)
    weights = jnp.concatenate([prefix, jnp.ones((CAP, CAP), jnp.bfloat16)], axis=1)
    lane6 = iota((SZ, CAP), 1)
    steps = [(0, 0, 0)] + [
        (dx, dy, dz) for dx in (-1, 0, 1) for dy in (-1, 0, 1) for dz in (-1, 0, 1) if (dx, dy, dz) != (0, 0, 0)
    ]

    def one_row(x, _):
        mine = [near[1, c, 1, x + 1] for c in range(3)]
        live = mine[0] < 0.5 * FAR
        low = [
            jnp.broadcast_to(jnp.min(mine[c], axis=1, keepdims=True) - REACH, (8, CAP)) for c in range(3)
        ]
        high = [
            jnp.broadcast_to(
                jnp.max(jnp.where(live, mine[c], -FAR), axis=1, keepdims=True) + REACH, (8, CAP)
            )
            for c in range(3)
        ]

        def neighbour(step):
            dx, dy, dz = step
            value = [near[dz + 1, c, dy + 1, x + 1 + dx] for c in range(3)]
            if dx:
                value[0] = value[0] + dx * SIDE[0]
            return value

        masks = []
        for step in steps:
            value = neighbour(step)
            tests = [value[c] <= high[c] if s > 0 else value[c] >= low[c] for c, s in enumerate(step) if s]
            if not any(s > 0 for s in step):
                tests.append(value[0] < 0.5 * FAR)
            hit = functools.reduce(jnp.logical_and, tests)
            masks.append(jnp.where(hit, 1.0, 0.0).astype(F32))
        ranks = jnp.dot(
            jnp.concatenate(masks, axis=0).astype(jnp.bfloat16), weights, preferred_element_type=F32
        )
        base = jnp.zeros((8, CAP), F32)
        for d, step in enumerate(steps):
            upto = ranks[8 * d : 8 * d + 8, :CAP]
            count = ranks[8 * d : 8 * d + 8, CAP:]
            base_int = base.astype(I32)
            want_int = (lane8 - base_int) & 127
            want = want_int.astype(F32)
            window = jnp.where(want < count, lax.shift_right_logical(base_int + want_int, 7), -1)
            at = jnp.zeros((8, CAP), I32)
            for width in (64, 32, 16, 8, 4, 2, 1):
                seen = jnp.take_along_axis(upto, at + (width - 1), axis=1)
                at = jnp.where(seen <= want, at + width, at)
            value = neighbour(step)
            packed[d, 3] = window.astype(F32)
            for c in range(3):
                packed[d, c] = jnp.take_along_axis(value[c], at & 127, axis=1)
            base = base + count
        total = base.astype(I32)
        used = jnp.max(jnp.where(live, lane8 + 1, 0).astype(F32), axis=1, keepdims=True).astype(I32)
        list_steps = lax.shift_right_logical(total + (128 * NL - 1), 7 + (NL - 1))
        row_steps = lax.shift_right_logical(jnp.broadcast_to(used, (8, CAP)) + (8 * ROWS - 1), 3 + {1: 0, 2: 1, 4: 2, 8: 3}[ROWS])
        totals[0] = list_steps
        totals[1] = row_steps
        longest = jnp.max(list_steps)

        def fill(t, _):
            tf = t.astype(F32)
            got = [jnp.full((8, CAP), FAR, F32)] * 3
            for d in range(NDIR):
                hit = packed[d, 3] == tf
                got = [jnp.where(hit, packed[d, c], got[c]) for c in range(3)]
            for c in range(3):
                lists[t, c] = got[c]
            return 0

        lax.fori_loop(0, longest * NL, fill, 0)

        columns[...] = jnp.concatenate(mine + [jnp.zeros((CAP - 24, CAP), F32)], axis=0).T
        force_columns[...] = jnp.zeros((CAP, CAP), F32)

        for z in range(SZ):
            n_list = totals[0, z, 0]
            n_rows = totals[1, z, 0]

            def row_group(g, _):
                start = pl.multiple_of(g * (8 * ROWS), 8 * ROWS)
                block = columns[pl.ds(start, 8 * ROWS), :]
                rows = [
                    [
                        jnp.broadcast_to(block[8 * i : 8 * i + 8, 8 * c + z : 8 * c + z + 1], (8, CAP))
                        for c in range(3)
                    ]
                    for i in range(ROWS)
                ]

                def list_step(t, sums):
                    sums = list(sums)
                    for u in range(NL):
                        other = [
                            jnp.broadcast_to(lists[t * NL + u, c, z : z + 1, :], (8, CAP)) for c in range(3)
                        ]
                        for i in range(ROWS):
                            delta = [rows[i][c] - other[c] for c in range(3)]
                            square = delta[0] * delta[0] + delta[1] * delta[1] + delta[2] * delta[2]
                            inside = (square < RC * RC) & (square > 0.0)
                            root = lax.rsqrt(jnp.where(inside, square, 1.0))
                            inverse = root * root
                            sixth = inverse * inverse * inverse
                            size = inverse * sixth * (48.0 * sixth - 24.0) - EDGE * root
                            size = jnp.where(inside, size, 0.0)
                            for c in range(3):
                                sums[3 * i + c] = sums[3 * i + c] + delta[c] * size
                    return tuple(sums)

                sums = lax.fori_loop(
                    0, n_list, list_step, tuple(jnp.zeros((8, CAP), F32) for _ in range(3 * ROWS))
                )
                for c in range(3):
                    column = jnp.concatenate(
                        [jnp.sum(sums[3 * i + c], axis=1, keepdims=True) for i in range(ROWS)], axis=0
                    )
                    force_columns[pl.ds(start, 8 * ROWS), 8 * c + z : 8 * c + z + 1] = column
                return 0

            lax.fori_loop(0, n_rows, row_group, 0)

        forces = force_columns[...].T
        for c in range(3):
            live6 = live[:SZ]
            force = jnp.where(live6, forces[8 * c : 8 * c + SZ], 0.0)
            out_forces[c, x] = force
            out_velocity[c, x] = vel[c, x] + 0.5 * STEP * force
            out_places[c, x] = jnp.where(live6, mine[c][:SZ], 0.0)
        return 0

    lax.fori_loop(0, SX, one_row, 0)


def per_device(sizes, places, velocity, forces_old, counts, mig_atom, mig_face):
    shape = places.shape
    flat = (3, SX, SZ, CAP)
    vmem = pl.BlockSpec(memory_space=pltpu.VMEM)
    smem = pl.BlockSpec(memory_space=pltpu.SMEM)
    dma = pltpu.SemaphoreType.DMA
    halo = pl.pallas_call(
        functools.partial(exchange_kernel, sizes),
        out_shape=[
            jax.ShapeDtypeStruct((3, SX, 8, CAP), F32),
            jax.ShapeDtypeStruct(flat, F32),
            jax.ShapeDtypeStruct((2, 3, SX, 8, CAP), F32),
            jax.ShapeDtypeStruct((3, 2, 3, 8, CAP), F32),
            jax.ShapeDtypeStruct((3, 2, 2, 3, 8, CAP), F32),
        ],
        in_specs=[smem] * 3 + [vmem] * 3,
        out_specs=[vmem] * 5,
        scratch_shapes=[
            pltpu.VMEM(flat, F32),
            pltpu.VMEM(flat, F32),
            pltpu.VMEM((8, CAP), F32),
            pltpu.VMEM((5, 8, CAP), F32),
            pltpu.VMEM((2, 3, 8, CAP), F32),
            dma((5,)), dma((5,)), dma((2,)), dma((2,)), dma((3, 2)), dma((3, 2)), dma((3, 2, 2)), dma((3, 2, 2)),
        ],
        compiler_params=pltpu.CompilerParams(collective_id=0, has_side_effects=True),
        name="exchange",
    )(counts, mig_atom, mig_face, places.reshape(flat), velocity.reshape(flat), forces_old.reshape(flat))
    outs = pl.pallas_call(
        force_kernel,
        out_shape=[jax.ShapeDtypeStruct(flat, F32)] * 3,
        in_specs=[vmem] * 5,
        out_specs=[vmem] * 3,
        scratch_shapes=[
            pltpu.VMEM((3, 3, 3, 8, 8, CAP), F32),
            pltpu.VMEM((NDIR, 4, 8, CAP), F32),
            pltpu.VMEM((NT, 3, 8, CAP), F32),
            pltpu.VMEM((CAP, CAP), F32),
            pltpu.VMEM((CAP, CAP), F32),
            pltpu.VMEM((2, 8, CAP), I32),
        ],
        name="forces",
    )(*halo)
    return tuple(out.reshape(shape) for out in outs)


def solution(mesh):
    sizes = tuple(mesh.shape[a] for a in ("gx", "gy", "gz"))
    block = P(None, "gx", "gy", "gz", None)
    moves = P("gx", "gy", "gz", None)
    return jax.shard_map(
        functools.partial(per_device, sizes),
        mesh=mesh,
        in_specs=(block, block, block, P("gx", "gy", "gz"), moves, moves),
        out_specs=(block, block, block),
        check_vma=False,
    )
```

```python
import functools

import jax
import jax.numpy as jnp
from jax import lax
from jax.experimental import pallas as pl
from jax.experimental.pallas import tpu as pltpu
from jax.sharding import PartitionSpec as P

MESH = pl.DeviceIdType.MESH
F32 = jnp.float32
I32 = jnp.int32
STEP = 0.005
RC = 2.5
SPACING = 1.1
EDGE = 24.0 * (2.0 * RC ** (-13) - RC ** (-7))
SIDE = (4.0 * SPACING, 4.0 * SPACING, SPACING * 8)
FAR = 1.0e4
REACH = RC * 1.0005
SX, SZ, CAP, MIG = 6, 6, 128, 16
NDIR = 27
ROWS = 4
NL = 2
NT = 32
GROUP = 8 * ROWS


def iota(shape, dim):
    return lax.broadcasted_iota(I32, shape, dim)


def exchange_kernel(sizes, counts, atoms, faces, places, velocity, forces,
                    own, vel, yblk, slab, zrow,
                    drift, half, letter, inbox, zsend,
                    lsend, lrecv, bsend, brecv, ssend, srecv, zs, zr):
    n_gx, n_gy, n_gz = sizes
    me = (lax.axis_index("gx"), lax.axis_index("gy"), lax.axis_index("gz"))

    def at(dx, dy, dz):
        return (
            lax.rem(me[0] + dx + n_gx, n_gx),
            lax.rem(me[1] + dy + n_gy, n_gy),
            lax.rem(me[2] + dz + n_gz, n_gz),
        )

    barrier = pltpu.get_barrier_semaphore()
    around = [
        (dx, dy, dz) for dx in (0, 1) for dy in (-1, 0, 1) for dz in (-1, 0, 1) if (dx, dy, dz) != (0, 0, 0)
    ]
    for step in around:
        pl.semaphore_signal(barrier, inc=1, device_id=at(*step), device_id_type=MESH)

    for c in range(3):
        for x in range(SX):
            h = velocity[c, x] + 0.5 * STEP * forces[c, x]
            half[c, x] = h
            drift[c, x] = places[c, x] + STEP * h

    sub8 = iota((8, CAP), 0)
    lane8 = iota((8, CAP), 1)
    lane1 = iota((1, CAP), 1)
    out_letter = jnp.where(sub8 == 6, -1.0, 0.0).astype(F32)
    leaving_cell = jnp.full((1, CAP), -1.0, F32)
    leaving_slot = jnp.full((1, CAP), -1.0, F32)
    for k in range(MIG):
        atom = atoms[0, 0, 0, k]
        face = faces[0, 0, 0, k]
        cell = lax.shift_right_logical(atom, 7)
        slot = atom & 127
        cx = lax.div(cell, SZ)
        cz = lax.rem(cell, SZ)
        axis = lax.shift_right_logical(face, 1)
        up = face & 1
        tile = jnp.zeros((8, CAP), F32)
        for c in range(6):
            source = drift if c < 3 else half
            row = source[c % 3, cx, pl.ds(cz, 1), :]
            tile = jnp.where(sub8 == c, jnp.broadcast_to(row, (8, CAP)), tile)
        column = jnp.sum(jnp.where(lane8 == slot, tile, 0.0), axis=1, keepdims=True)
        sign = (2 * up - 1).astype(F32)
        shift = jnp.where(axis == 2, SIDE[2], SIDE[0]).astype(F32) * sign
        sub_col = iota((8, 1), 0)
        column = column - jnp.where(sub_col == axis, shift, 0.0)
        nx = jnp.where(axis == 0, (1 - up) * (SX - 1), cx)
        nz = jnp.where(axis == 2, (1 - up) * (SZ - 1), cz)
        column = jnp.where(sub_col == 6, (nx * 8 + nz).astype(F32), column)
        out_letter = jnp.where(lane8 == 16 * (face ^ 1) + k, column, out_letter)
        leaving_cell = jnp.where(lane1 == 96 + k, (cx * 8 + cz).astype(F32), leaving_cell)
        leaving_slot = jnp.where(lane1 == 96 + k, slot.astype(F32), leaving_slot)
    letter[...] = out_letter

    pl.semaphore_wait(barrier, len(around))

    posts = []
    for box, step in enumerate(((1, 0, 0), (0, 1, 0), (0, -1, 0), (0, 0, 1), (0, 0, -1))):
        post = pltpu.make_async_remote_copy(
            src_ref=letter, dst_ref=inbox.at[box], send_sem=lsend.at[box], recv_sem=lrecv.at[box],
            device_id=at(*step), device_id_type=MESH,
        )
        post.start()
        posts.append(post)

    count_rows = []
    for x in range(SX):
        row = jnp.zeros((8, CAP), I32)
        for z in range(SZ):
            row = jnp.where(sub8 == z, counts[x, 0, z], row)
        count_rows.append(row)

    for post in posts:
        post.wait_recv()
    got = inbox[4]
    for box, top in ((3, 80), (2, 64), (1, 48), (0, 32)):
        got = jnp.where(lane8 < top, inbox[box], got)
    arriving_cell = jnp.where(lane1 < 96, got[6:7, :], -1.0)
    sub8f = sub8.astype(F32)
    here = []
    gone = []
    for x in range(SX):
        here.append((jnp.broadcast_to(arriving_cell, (8, CAP)) == sub8f + 8.0 * x).astype(F32))
        gone.append((jnp.broadcast_to(leaving_cell, (8, CAP)) == sub8f + 8.0 * x).astype(F32))
    here_all = jnp.concatenate(here, axis=0)
    gone_all = jnp.concatenate(gone, axis=0)
    earlier = (iota((CAP, CAP), 0) < iota((CAP, CAP), 1)).astype(jnp.bfloat16)
    rank = jnp.dot(here_all.astype(jnp.bfloat16), earlier, preferred_element_type=F32)
    slot_table = here_all * (rank + jnp.concatenate(count_rows, axis=0).astype(F32))
    target = jnp.sum(slot_table, axis=0, keepdims=True)
    target = jnp.where(lane1 < 96, target, leaving_slot)
    slot_hit = (jnp.broadcast_to(target, (CAP, CAP)) == iota((CAP, CAP), 0).astype(F32)).astype(jnp.bfloat16)
    pieces = [(here_all - gone_all).astype(jnp.bfloat16)]
    for c in range(6):
        part = here_all * jnp.broadcast_to(jnp.where(lane1 < 96, got[c : c + 1, :], 0.0), here_all.shape)
        for _ in range(3):
            top = part.astype(jnp.bfloat16)
            pieces.append(top)
            part = part - top.astype(F32)
    landed = lax.dot_general(
        jnp.concatenate(pieces, axis=0), slot_hit, (((1,), (1,)), ((), ())), preferred_element_type=F32
    )
    n = SX * 8

    def arrived(c, x):
        base = n * (1 + 3 * c) + 8 * x
        return (
            landed[base : base + SZ] + landed[base + n : base + n + SZ] + landed[base + 2 * n : base + 2 * n + SZ]
        )

    lane6 = iota((SZ, CAP), 1)
    for x in range(SX):
        delta = landed[8 * x : 8 * x + SZ]
        live = (lane6 < count_rows[x][:SZ]).astype(F32) + delta > 0.5
        came = delta > 0.5
        for c in range(3):
            place = jnp.where(came, arrived(c, x), drift[c, x])
            place = jnp.where(live, place, FAR)
            own[c, x, 0:SZ] = place
            own[c, x, SZ:8] = jnp.full((8 - SZ, CAP), FAR, F32)
            zsend[0, c, x : x + 1] = place[0:1]
            zsend[1, c, x : x + 1] = place[SZ - 1 : SZ]
            speed = jnp.where(came, arrived(3 + c, x), half[c, x])
            vel[c, x] = jnp.where(live, speed, 0.0)
    for side in range(2):
        for c in range(3):
            zsend[side, c, SX:8] = jnp.full((8 - SX, CAP), FAR, F32)

    copies = []

    def send(src, dst, ssem, rsem, step):
        copy = pltpu.make_async_remote_copy(
            src_ref=src, dst_ref=dst, send_sem=ssem, recv_sem=rsem, device_id=at(*step), device_id_type=MESH
        )
        copy.start()
        copies.append(copy)

    for i, dy in enumerate((1, -1)):
        send(own, yblk.at[i], bsend.at[i], brecv.at[i], (0, dy, 0))
    for dy in (1, -1, 0):
        there = 1 - dy
        for s, x in ((0, 0), (1, SX - 1)):
            send(own.at[:, x], slab.at[there, s], ssend.at[there, s], srecv.at[there, s], (1, dy, 0))
    for dy in (1, -1, 0):
        there = 1 - dy
        for dx in (0, 1):
            for zi, dz in ((0, -1), (1, 1)):
                send(zsend.at[zi], zrow.at[there, dx, 1 - zi], zs.at[there, dx, zi], zr.at[there, dx, 1 - zi], (dx, dy, dz))
    for post in posts:
        post.wait_send()
    for copy in copies:
        copy.wait_send()
    for i, dy in enumerate((1, -1)):
        pltpu.make_async_remote_copy(
            src_ref=own, dst_ref=yblk.at[i], send_sem=bsend.at[i], recv_sem=brecv.at[i],
            device_id=at(0, dy, 0), device_id_type=MESH).wait_recv()
    for y in range(3):
        for s in range(2):
            pltpu.make_async_remote_copy(
                src_ref=own.at[:, 0], dst_ref=slab.at[y, s], send_sem=ssend.at[y, s], recv_sem=srecv.at[y, s],
                device_id=at(1, 0, 0), device_id_type=MESH).wait_recv()
        for g in range(2):
            for s in range(2):
                pltpu.make_async_remote_copy(
                    src_ref=zsend.at[0], dst_ref=zrow.at[y, g, s], send_sem=zs.at[y, g, s], recv_sem=zr.at[y, g, s],
                    device_id=at(0, 0, 1), device_id_type=MESH).wait_recv()


def force_kernel(own, vel, yblk, slab, zrow, out_places, out_velocity, out_forces,
                 near, packed, lists, columns, force_columns, splat, sums_of, totals):
    sub8 = iota((8, CAP), 0)
    lane8 = iota((8, CAP), 1)

    for y in range(3):
        for c in range(3):
            for xi in range(8):
                if xi == 0:
                    tile = slab[y, 1, c]
                    low, high = (zrow[y, 1, s, c, SX - 1 : SX] for s in (0, 1))
                elif xi == 7:
                    tile = slab[y, 0, c]
                    low, high = (zrow[y, 1, s, c, 0:1] for s in (0, 1))
                else:
                    tile = own[c, xi - 1] if y == 1 else yblk[y // 2, c, xi - 1]
                    low, high = (zrow[y, 0, s, c, xi - 1 : xi] for s in (0, 1))
                below = jnp.where(sub8 == 0, jnp.broadcast_to(low, (8, CAP)), pltpu.roll(tile, 1, 0))
                above = jnp.where(sub8 == SZ - 1, jnp.broadcast_to(high, (8, CAP)), pltpu.roll(tile, 7, 0))
                for zi, value in enumerate((below, tile, above)):
                    if c == 1 and y != 1:
                        value = value + (y - 1) * SIDE[1]
                    if c == 2 and zi != 1:
                        value = value + (zi - 1) * SIDE[2]
                    near[zi, c, y, xi] = value

    prefix = (iota((CAP, CAP), 0) <= iota((CAP, CAP), 1)).astype(jnp.bfloat16)
    weights = jnp.concatenate([prefix, jnp.ones((CAP, CAP), jnp.bfloat16)], axis=1)
    lane6 = iota((SZ, CAP), 1)
    steps = [(0, 0, 0)] + [
        (dx, dy, dz) for dx in (-1, 0, 1) for dy in (-1, 0, 1) for dz in (-1, 0, 1) if (dx, dy, dz) != (0, 0, 0)
    ]

    def one_row(x, _):
        mine = [near[1, c, 1, x + 1] for c in range(3)]
        live = mine[0] < 0.5 * FAR
        low = [
            jnp.broadcast_to(jnp.min(mine[c], axis=1, keepdims=True), (8, CAP)) for c in range(3)
        ]
        high = [
            jnp.broadcast_to(
                jnp.max(jnp.where(live, mine[c], -FAR), axis=1, keepdims=True), (8, CAP)
            )
            for c in range(3)
        ]

        def neighbour(step):
            dx, dy, dz = step
            value = [near[dz + 1, c, dy + 1, x + 1 + dx] for c in range(3)]
            if dx:
                value[0] = value[0] + dx * SIDE[0]
            return value

        masks = []
        for step in steps:
            value = neighbour(step)
            gaps = [value[c] - high[c] if s > 0 else low[c] - value[c] for c, s in enumerate(step) if s]
            if len(gaps) > 1:
                gaps = [jnp.maximum(gap, 0.0) for gap in gaps]
                hit = sum(gap * gap for gap in gaps) < REACH * REACH
            elif gaps:
                hit = gaps[0] < REACH
            if not any(s > 0 for s in step):
                alive = value[0] < 0.5 * FAR
                hit = hit & alive if gaps else alive
            masks.append(jnp.where(hit, 1.0, 0.0).astype(F32))
        ranks = jnp.dot(
            jnp.concatenate(masks, axis=0).astype(jnp.bfloat16), weights, preferred_element_type=F32
        )
        base = jnp.zeros((8, CAP), F32)
        for d, step in enumerate(steps):
            upto = ranks[8 * d : 8 * d + 8, :CAP]
            count = ranks[8 * d : 8 * d + 8, CAP:]
            base_int = base.astype(I32)
            want_int = (lane8 - base_int) & 127
            want = want_int.astype(F32)
            window = jnp.where(want < count, lax.shift_right_logical(base_int + want_int, 7), -1)
            at = jnp.zeros((8, CAP), I32)
            for width in (64, 32, 16, 8, 4, 2, 1):
                seen = jnp.take_along_axis(upto, at + (width - 1), axis=1)
                at = jnp.where(seen <= want, at + width, at)
            value = neighbour(step)
            packed[d, 3] = window.astype(F32)
            for c in range(3):
                packed[d, c] = jnp.take_along_axis(value[c], at & 127, axis=1)
            base = base + count
        total = base.astype(I32)
        used = jnp.max(jnp.where(live, lane8 + 1, 0).astype(F32), axis=1, keepdims=True).astype(I32)
        list_steps = lax.shift_right_logical(total + (128 * NL - 1), 7 + (NL - 1))
        row_steps = lax.shift_right_logical(jnp.broadcast_to(used, (8, CAP)) + (8 * ROWS - 1), 3 + {1: 0, 2: 1, 4: 2, 8: 3}[ROWS])
        totals[0] = list_steps
        totals[1] = row_steps
        longest = jnp.max(list_steps)

        def fill(t, _):
            tf = t.astype(F32)
            got = [jnp.full((8, CAP), FAR, F32)] * 3
            for d in range(NDIR):
                hit = packed[d, 3] == tf
                got = [jnp.where(hit, packed[d, c], got[c]) for c in range(3)]
            for c in range(3):
                lists[t, c] = got[c]
            return 0

        lax.fori_loop(0, longest * NL, fill, 0)

        columns[...] = jnp.concatenate(mine + [jnp.zeros((CAP - 24, CAP), F32)], axis=0).T
        most_groups = jnp.max(row_steps)

        def spread(g, _):
            start = pl.multiple_of(g * GROUP, GROUP)
            block = columns[pl.ds(start, GROUP), :]
            for z in range(SZ):
                for c in range(3):
                    splat[3 * z + c, pl.ds(start, GROUP), :] = jnp.broadcast_to(
                        block[:, 8 * c + z : 8 * c + z + 1], (GROUP, CAP)
                    )
            return 0

        lax.fori_loop(0, most_groups, spread, 0)

        for z in range(SZ):
            n_list = totals[0, z, 0]
            n_rows = totals[1, z, 0]

            def row_group(g, _):
                start = pl.multiple_of(g * GROUP, GROUP)

                def list_step(t, sums):
                    sums = list(sums)
                    for u in range(NL):
                        other = [
                            jnp.broadcast_to(lists[t * NL + u, c, z : z + 1, :], (8, CAP)) for c in range(3)
                        ]
                        for i in range(ROWS):
                            rows = pl.ds(pl.multiple_of(start + 8 * i, 8), 8)
                            delta = [splat[3 * z + c, rows, :] - other[c] for c in range(3)]
                            square = delta[0] * delta[0] + delta[1] * delta[1] + delta[2] * delta[2]
                            root = lax.rsqrt(jnp.maximum(square, 0.01))
                            second = root * root
                            sixth = second * second * second
                            size = root * ((root * sixth) * (sixth - 0.5) - EDGE / 48.0)
                            size = jnp.where(square < RC * RC, size, 0.0)
                            for c in range(3):
                                sums[3 * i + c] = sums[3 * i + c] + delta[c] * size
                    return tuple(sums)

                sums = lax.fori_loop(
                    0, n_list, list_step, tuple(jnp.zeros((8, CAP), F32) for _ in range(3 * ROWS))
                )
                for i in range(ROWS):
                    for c in range(3):
                        rows = pl.ds(pl.multiple_of(start + 8 * i, 8), 8)
                        sums_of[3 * z + c, rows, :] = sums[3 * i + c]
                return 0

            lax.fori_loop(0, n_rows, row_group, 0)

        def gather_sums(g, _):
            start = pl.multiple_of(g * GROUP, GROUP)
            for i in range(ROWS):
                rows = pl.ds(pl.multiple_of(start + 8 * i, 8), 8)
                block = jnp.zeros((8, CAP), F32)
                for z in range(SZ):
                    for c in range(3):
                        total = jnp.sum(sums_of[3 * z + c, rows, :], axis=1, keepdims=True)
                        block = jnp.where(lane8 == 8 * c + z, total, block)
                force_columns[rows, :] = block
            return 0

        lax.fori_loop(0, most_groups, gather_sums, 0)

        forces = force_columns[...].T
        for c in range(3):
            live6 = live[:SZ]
            force = jnp.where(live6, 48.0 * forces[8 * c : 8 * c + SZ], 0.0)
            out_forces[c, x] = force
            out_velocity[c, x] = vel[c, x] + 0.5 * STEP * force
            out_places[c, x] = jnp.where(live6, mine[c][:SZ], 0.0)
        return 0

    lax.fori_loop(0, SX, one_row, 0)


def per_device(sizes, places, velocity, forces_old, counts, mig_atom, mig_face):
    shape = places.shape
    flat = (3, SX, SZ, CAP)
    vmem = pl.BlockSpec(memory_space=pltpu.VMEM)
    smem = pl.BlockSpec(memory_space=pltpu.SMEM)
    dma = pltpu.SemaphoreType.DMA
    halo = pl.pallas_call(
        functools.partial(exchange_kernel, sizes),
        out_shape=[
            jax.ShapeDtypeStruct((3, SX, 8, CAP), F32),
            jax.ShapeDtypeStruct(flat, F32),
            jax.ShapeDtypeStruct((2, 3, SX, 8, CAP), F32),
            jax.ShapeDtypeStruct((3, 2, 3, 8, CAP), F32),
            jax.ShapeDtypeStruct((3, 2, 2, 3, 8, CAP), F32),
        ],
        in_specs=[smem] * 3 + [vmem] * 3,
        out_specs=[vmem] * 5,
        scratch_shapes=[
            pltpu.VMEM(flat, F32),
            pltpu.VMEM(flat, F32),
            pltpu.VMEM((8, CAP), F32),
            pltpu.VMEM((5, 8, CAP), F32),
            pltpu.VMEM((2, 3, 8, CAP), F32),
            dma((5,)), dma((5,)), dma((2,)), dma((2,)), dma((3, 2)), dma((3, 2)), dma((3, 2, 2)), dma((3, 2, 2)),
        ],
        compiler_params=pltpu.CompilerParams(collective_id=0, has_side_effects=True),
        name="exchange",
    )(counts, mig_atom, mig_face, places.reshape(flat), velocity.reshape(flat), forces_old.reshape(flat))
    outs = pl.pallas_call(
        force_kernel,
        out_shape=[jax.ShapeDtypeStruct(flat, F32)] * 3,
        in_specs=[vmem] * 5,
        out_specs=[vmem] * 3,
        scratch_shapes=[
            pltpu.VMEM((3, 3, 3, 8, 8, CAP), F32),
            pltpu.VMEM((NDIR, 4, 8, CAP), F32),
            pltpu.VMEM((NT, 3, 8, CAP), F32),
            pltpu.VMEM((CAP, CAP), F32),
            pltpu.VMEM((CAP, CAP), F32),
            pltpu.VMEM((3 * SZ, CAP, CAP), F32),
            pltpu.VMEM((3 * SZ, CAP, CAP), F32),
            pltpu.VMEM((2, 8, CAP), I32),
        ],
        name="forces",
    )(*halo)
    return tuple(out.reshape(shape) for out in outs)


def solution(mesh):
    sizes = tuple(mesh.shape[a] for a in ("gx", "gy", "gz"))
    block = P(None, "gx", "gy", "gz", None)
    moves = P("gx", "gy", "gz", None)
    return jax.shard_map(
        functools.partial(per_device, sizes),
        mesh=mesh,
        in_specs=(block, block, block, P("gx", "gy", "gz"), moves, moves),
        out_specs=(block, block, block),
        check_vma=False,
    )
```

```python
import functools

import jax
import jax.numpy as jnp
from jax import lax
from jax.experimental import pallas as pl
from jax.experimental.pallas import tpu as pltpu
from jax.sharding import PartitionSpec as P

MESH = pl.DeviceIdType.MESH
F32 = jnp.float32
I32 = jnp.int32
STEP = 0.005
RC = 2.5
SPACING = 1.1
EDGE = 24.0 * (2.0 * RC ** (-13) - RC ** (-7))
SIDE = (4.0 * SPACING, 4.0 * SPACING, SPACING * 8)
FAR = 1.0e4
REACH = RC * 1.0005
SX, SZ, CAP, MIG = 6, 6, 128, 16
NDIR = 27
ROWS = 4
NL = 2
NT = 32
GROUP = 8 * ROWS


def iota(shape, dim):
    return lax.broadcasted_iota(I32, shape, dim)


def exchange_kernel(sizes, counts_in, atoms_in, faces_in, places_in, velocity_in, forces_in,
                    own, vel, yblk, slab, zrow,
                    counts, atoms, faces, places, velocity, forces, load_sem, drift, half, letter, inbox, zsend,
                    lsend, lrecv, bsend, brecv, ssend, srecv, zs, zr):
    n_gx, n_gy, n_gz = sizes
    me = (lax.axis_index("gx"), lax.axis_index("gy"), lax.axis_index("gz"))

    def at(dx, dy, dz):
        return (
            lax.rem(me[0] + dx + n_gx, n_gx),
            lax.rem(me[1] + dy + n_gy, n_gy),
            lax.rem(me[2] + dz + n_gz, n_gz),
        )

    barrier = pltpu.get_barrier_semaphore()
    around = [
        (dx, dy, dz) for dx in (0, 1) for dy in (-1, 0, 1) for dz in (-1, 0, 1) if (dx, dy, dz) != (0, 0, 0)
    ]
    for step in around:
        pl.semaphore_signal(barrier, inc=1, device_id=at(*step), device_id_type=MESH)

    loads = [
        pltpu.make_async_copy(src, dst, load_sem.at[i])
        for i, (src, dst) in enumerate((
            (places_in, places), (velocity_in, velocity), (forces_in, forces),
            (atoms_in, atoms), (faces_in, faces), (counts_in, counts),
        ))
    ]
    for load in loads:
        load.start()
    for load in loads:
        load.wait()
    for c in range(3):
        for x in range(SX):
            rows = slice(SZ * (SX * c + x), SZ * (SX * c + x) + SZ)
            h = velocity[rows, 0, :] + 0.5 * STEP * forces[rows, 0, :]
            half[c, x] = h
            drift[c, x] = places[rows, 0, :] + STEP * h

    sub8 = iota((8, CAP), 0)
    lane8 = iota((8, CAP), 1)
    lane1 = iota((1, CAP), 1)
    out_letter = jnp.where(sub8 == 6, -1.0, 0.0).astype(F32)
    leaving_cell = jnp.full((1, CAP), -1.0, F32)
    leaving_slot = jnp.full((1, CAP), -1.0, F32)
    for k in range(MIG):
        atom = atoms[0, 0, 0, k]
        face = faces[0, 0, 0, k]
        cell = lax.shift_right_logical(atom, 7)
        slot = atom & 127
        cx = lax.div(cell, SZ)
        cz = lax.rem(cell, SZ)
        axis = lax.shift_right_logical(face, 1)
        up = face & 1
        tile = jnp.zeros((8, CAP), F32)
        for c in range(6):
            source = drift if c < 3 else half
            row = source[c % 3, cx, pl.ds(cz, 1), :]
            tile = jnp.where(sub8 == c, jnp.broadcast_to(row, (8, CAP)), tile)
        column = jnp.sum(jnp.where(lane8 == slot, tile, 0.0), axis=1, keepdims=True)
        sign = (2 * up - 1).astype(F32)
        shift = jnp.where(axis == 2, SIDE[2], SIDE[0]).astype(F32) * sign
        sub_col = iota((8, 1), 0)
        column = column - jnp.where(sub_col == axis, shift, 0.0)
        nx = jnp.where(axis == 0, (1 - up) * (SX - 1), cx)
        nz = jnp.where(axis == 2, (1 - up) * (SZ - 1), cz)
        column = jnp.where(sub_col == 6, (nx * 8 + nz).astype(F32), column)
        out_letter = jnp.where(lane8 == 16 * (face ^ 1) + k, column, out_letter)
        leaving_cell = jnp.where(lane1 == 96 + k, (cx * 8 + cz).astype(F32), leaving_cell)
        leaving_slot = jnp.where(lane1 == 96 + k, slot.astype(F32), leaving_slot)
    letter[...] = out_letter

    pl.semaphore_wait(barrier, len(around))

    posts = []
    for box, step in enumerate(((1, 0, 0), (0, 1, 0), (0, -1, 0), (0, 0, 1), (0, 0, -1))):
        post = pltpu.make_async_remote_copy(
            src_ref=letter, dst_ref=inbox.at[box], send_sem=lsend.at[box], recv_sem=lrecv.at[box],
            device_id=at(*step), device_id_type=MESH,
        )
        post.start()
        posts.append(post)

    count_rows = []
    for x in range(SX):
        row = jnp.zeros((8, CAP), I32)
        for z in range(SZ):
            row = jnp.where(sub8 == z, counts[x, 0, z], row)
        count_rows.append(row)

    for post in posts:
        post.wait_recv()
    got = inbox[4]
    for box, top in ((3, 80), (2, 64), (1, 48), (0, 32)):
        got = jnp.where(lane8 < top, inbox[box], got)
    arriving_cell = jnp.where(lane1 < 96, got[6:7, :], -1.0)
    sub8f = sub8.astype(F32)
    here = []
    gone = []
    for x in range(SX):
        here.append((jnp.broadcast_to(arriving_cell, (8, CAP)) == sub8f + 8.0 * x).astype(F32))
        gone.append((jnp.broadcast_to(leaving_cell, (8, CAP)) == sub8f + 8.0 * x).astype(F32))
    here_all = jnp.concatenate(here, axis=0)
    gone_all = jnp.concatenate(gone, axis=0)
    earlier = (iota((CAP, CAP), 0) < iota((CAP, CAP), 1)).astype(jnp.bfloat16)
    rank = jnp.dot(here_all.astype(jnp.bfloat16), earlier, preferred_element_type=F32)
    slot_table = here_all * (rank + jnp.concatenate(count_rows, axis=0).astype(F32))
    target = jnp.sum(slot_table, axis=0, keepdims=True)
    target = jnp.where(lane1 < 96, target, leaving_slot)
    slot_hit = (jnp.broadcast_to(target, (CAP, CAP)) == iota((CAP, CAP), 0).astype(F32)).astype(jnp.bfloat16)
    pieces = [(here_all - gone_all).astype(jnp.bfloat16)]
    for c in range(6):
        part = here_all * jnp.broadcast_to(jnp.where(lane1 < 96, got[c : c + 1, :], 0.0), here_all.shape)
        for _ in range(3):
            top = part.astype(jnp.bfloat16)
            pieces.append(top)
            part = part - top.astype(F32)
    landed = lax.dot_general(
        jnp.concatenate(pieces, axis=0), slot_hit, (((1,), (1,)), ((), ())), preferred_element_type=F32
    )
    n = SX * 8

    def arrived(c, x):
        base = n * (1 + 3 * c) + 8 * x
        return (
            landed[base : base + SZ] + landed[base + n : base + n + SZ] + landed[base + 2 * n : base + 2 * n + SZ]
        )

    lane6 = iota((SZ, CAP), 1)
    for x in range(SX):
        delta = landed[8 * x : 8 * x + SZ]
        live = (lane6 < count_rows[x][:SZ]).astype(F32) + delta > 0.5
        came = delta > 0.5
        for c in range(3):
            place = jnp.where(came, arrived(c, x), drift[c, x])
            place = jnp.where(live, place, FAR)
            own[c, x, 0:SZ] = place
            own[c, x, SZ:8] = jnp.full((8 - SZ, CAP), FAR, F32)
            zsend[0, c, x : x + 1] = place[0:1]
            zsend[1, c, x : x + 1] = place[SZ - 1 : SZ]
            speed = jnp.where(came, arrived(3 + c, x), half[c, x])
            vel[c, x] = jnp.where(live, speed, 0.0)
    for side in range(2):
        for c in range(3):
            zsend[side, c, SX:8] = jnp.full((8 - SX, CAP), FAR, F32)

    copies = []

    def send(src, dst, ssem, rsem, step):
        copy = pltpu.make_async_remote_copy(
            src_ref=src, dst_ref=dst, send_sem=ssem, recv_sem=rsem, device_id=at(*step), device_id_type=MESH
        )
        copy.start()
        copies.append(copy)

    for dy in (1, -1, 0):
        there = 1 - dy
        for dx in (1, 0):
            for zi, dz in ((0, -1), (1, 1)):
                send(zsend.at[zi], zrow.at[there, dx, 1 - zi], zs.at[there, dx, zi], zr.at[there, dx, 1 - zi], (dx, dy, dz))
    for i, dy in enumerate((1, -1)):
        send(own, yblk.at[i], bsend.at[i], brecv.at[i], (0, dy, 0))
    for dy in (1, -1, 0):
        there = 1 - dy
        for s, x in ((0, 0), (1, SX - 1)):
            send(own.at[:, x], slab.at[there, s], ssend.at[there, s], srecv.at[there, s], (1, dy, 0))
    for post in posts:
        post.wait_send()
    for copy in copies:
        copy.wait_send()
    for i, dy in enumerate((1, -1)):
        pltpu.make_async_remote_copy(
            src_ref=own, dst_ref=yblk.at[i], send_sem=bsend.at[i], recv_sem=brecv.at[i],
            device_id=at(0, dy, 0), device_id_type=MESH).wait_recv()
    for y in range(3):
        for s in range(2):
            pltpu.make_async_remote_copy(
                src_ref=own.at[:, 0], dst_ref=slab.at[y, s], send_sem=ssend.at[y, s], recv_sem=srecv.at[y, s],
                device_id=at(1, 0, 0), device_id_type=MESH).wait_recv()
        for g in range(2):
            for s in range(2):
                pltpu.make_async_remote_copy(
                    src_ref=zsend.at[0], dst_ref=zrow.at[y, g, s], send_sem=zs.at[y, g, s], recv_sem=zr.at[y, g, s],
                    device_id=at(0, 0, 1), device_id_type=MESH).wait_recv()


def force_kernel(own, vel, yblk, slab, zrow, out_places, out_velocity, out_forces,
                 near, packed, lists, columns, force_columns, splat, sums_of, totals,
                 places_rows, velocity_rows, forces_rows, store_sem):
    sub8 = iota((8, CAP), 0)
    lane8 = iota((8, CAP), 1)

    for y in range(3):
        for c in range(3):
            for xi in range(8):
                if xi == 0:
                    tile = slab[y, 1, c]
                    low, high = (zrow[y, 1, s, c, SX - 1 : SX] for s in (0, 1))
                elif xi == 7:
                    tile = slab[y, 0, c]
                    low, high = (zrow[y, 1, s, c, 0:1] for s in (0, 1))
                else:
                    tile = own[c, xi - 1] if y == 1 else yblk[y // 2, c, xi - 1]
                    low, high = (zrow[y, 0, s, c, xi - 1 : xi] for s in (0, 1))
                below = jnp.where(sub8 == 0, jnp.broadcast_to(low, (8, CAP)), pltpu.roll(tile, 1, 0))
                above = jnp.where(sub8 == SZ - 1, jnp.broadcast_to(high, (8, CAP)), pltpu.roll(tile, 7, 0))
                for zi, value in enumerate((below, tile, above)):
                    if c == 1 and y != 1:
                        value = value + (y - 1) * SIDE[1]
                    if c == 2 and zi != 1:
                        value = value + (zi - 1) * SIDE[2]
                    near[zi, c, y, xi] = value

    prefix = (iota((CAP, CAP), 0) <= iota((CAP, CAP), 1)).astype(jnp.bfloat16)
    weights = jnp.concatenate([prefix, jnp.ones((CAP, CAP), jnp.bfloat16)], axis=1)
    lane6 = iota((SZ, CAP), 1)
    steps = [(0, 0, 0)] + [
        (dx, dy, dz) for dx in (-1, 0, 1) for dy in (-1, 0, 1) for dz in (-1, 0, 1) if (dx, dy, dz) != (0, 0, 0)
    ]

    stores = ((places_rows, out_places), (velocity_rows, out_velocity), (forces_rows, out_forces))

    def one_row(x, _):
        mine = [near[1, c, 1, x + 1] for c in range(3)]
        live = mine[0] < 0.5 * FAR
        low = [
            jnp.broadcast_to(jnp.min(mine[c], axis=1, keepdims=True), (8, CAP)) for c in range(3)
        ]
        high = [
            jnp.broadcast_to(
                jnp.max(jnp.where(live, mine[c], -FAR), axis=1, keepdims=True), (8, CAP)
            )
            for c in range(3)
        ]

        def neighbour(step):
            dx, dy, dz = step
            value = [near[dz + 1, c, dy + 1, x + 1 + dx] for c in range(3)]
            if dx:
                value[0] = value[0] + dx * SIDE[0]
            return value

        masks = []
        for step in steps:
            value = neighbour(step)
            gaps = [value[c] - high[c] if s > 0 else low[c] - value[c] for c, s in enumerate(step) if s]
            if len(gaps) > 1:
                gaps = [jnp.maximum(gap, 0.0) for gap in gaps]
                hit = sum(gap * gap for gap in gaps) < REACH * REACH
            elif gaps:
                hit = gaps[0] < REACH
            if not any(s > 0 for s in step):
                alive = value[0] < 0.5 * FAR
                hit = hit & alive if gaps else alive
            masks.append(jnp.where(hit, 1.0, 0.0).astype(F32))
        ranks = jnp.dot(
            jnp.concatenate(masks, axis=0).astype(jnp.bfloat16), weights, preferred_element_type=F32
        )
        base = jnp.zeros((8, CAP), F32)
        for d, step in enumerate(steps):
            upto = ranks[8 * d : 8 * d + 8, :CAP]
            count = ranks[8 * d : 8 * d + 8, CAP:]
            base_int = base.astype(I32)
            want_int = (lane8 - base_int) & 127
            want = want_int.astype(F32)
            window = jnp.where(want < count, lax.shift_right_logical(base_int + want_int, 7), -1)
            at = jnp.zeros((8, CAP), I32)
            for width in (64, 32, 16, 8, 4, 2, 1):
                seen = jnp.take_along_axis(upto, at + (width - 1), axis=1)
                at = jnp.where(seen <= want, at + width, at)
            value = neighbour(step)
            packed[d, 3] = window.astype(F32)
            for c in range(3):
                packed[d, c] = jnp.take_along_axis(value[c], at & 127, axis=1)
            base = base + count
        total = base.astype(I32)
        used = jnp.max(jnp.where(live, lane8 + 1, 0).astype(F32), axis=1, keepdims=True).astype(I32)
        list_steps = lax.shift_right_logical(total + (128 * NL - 1), 7 + (NL - 1))
        row_steps = lax.shift_right_logical(jnp.broadcast_to(used, (8, CAP)) + (8 * ROWS - 1), 3 + {1: 0, 2: 1, 4: 2, 8: 3}[ROWS])
        totals[0] = list_steps
        totals[1] = row_steps
        longest = jnp.max(list_steps)

        def fill(t, _):
            tf = t.astype(F32)
            got = [jnp.full((8, CAP), FAR, F32)] * 3
            for d in range(NDIR):
                hit = packed[d, 3] == tf
                got = [jnp.where(hit, packed[d, c], got[c]) for c in range(3)]
            for c in range(3):
                lists[t, c] = got[c]
            return 0

        lax.fori_loop(0, longest * NL, fill, 0)

        columns[...] = jnp.concatenate(mine + [jnp.zeros((CAP - 24, CAP), F32)], axis=0).T
        most_groups = jnp.max(row_steps)

        def spread(g, _):
            start = pl.multiple_of(g * GROUP, GROUP)
            block = columns[pl.ds(start, GROUP), :]
            for z in range(SZ):
                for c in range(3):
                    splat[3 * z + c, pl.ds(start, GROUP), :] = jnp.broadcast_to(
                        block[:, 8 * c + z : 8 * c + z + 1], (GROUP, CAP)
                    )
            return 0

        lax.fori_loop(0, most_groups, spread, 0)

        for z in range(SZ):
            n_list = totals[0, z, 0]
            n_rows = totals[1, z, 0]

            def row_group(g, _):
                start = pl.multiple_of(g * GROUP, GROUP)

                def list_step(t, sums):
                    sums = list(sums)
                    for u in range(NL):
                        other = [
                            jnp.broadcast_to(lists[t * NL + u, c, z : z + 1, :], (8, CAP)) for c in range(3)
                        ]
                        for i in range(ROWS):
                            rows = pl.ds(pl.multiple_of(start + 8 * i, 8), 8)
                            delta = [splat[3 * z + c, rows, :] - other[c] for c in range(3)]
                            square = delta[0] * delta[0] + delta[1] * delta[1] + delta[2] * delta[2]
                            root = lax.rsqrt(jnp.maximum(square, 0.01))
                            second = root * root
                            sixth = second * second * second
                            size = root * ((root * sixth) * (sixth - 0.5) - EDGE / 48.0)
                            size = jnp.where(square < RC * RC, size, 0.0)
                            for c in range(3):
                                sums[3 * i + c] = sums[3 * i + c] + delta[c] * size
                    return tuple(sums)

                sums = lax.fori_loop(
                    0, n_list, list_step, tuple(jnp.zeros((8, CAP), F32) for _ in range(3 * ROWS))
                )
                for i in range(ROWS):
                    for c in range(3):
                        rows = pl.ds(pl.multiple_of(start + 8 * i, 8), 8)
                        sums_of[3 * z + c, rows, :] = sums[3 * i + c]
                return 0

            lax.fori_loop(0, n_rows, row_group, 0)

        def gather_sums(g, _):
            start = pl.multiple_of(g * GROUP, GROUP)
            for i in range(ROWS):
                rows = pl.ds(pl.multiple_of(start + 8 * i, 8), 8)
                block = jnp.zeros((8, CAP), F32)
                for z in range(SZ):
                    for c in range(3):
                        total = jnp.sum(sums_of[3 * z + c, rows, :], axis=1, keepdims=True)
                        block = jnp.where(lane8 == 8 * c + z, total, block)
                force_columns[rows, :] = block
            return 0

        lax.fori_loop(0, most_groups, gather_sums, 0)

        forces = force_columns[...].T
        for c in range(3):
            live6 = live[:SZ]
            force = jnp.where(live6, 48.0 * forces[8 * c : 8 * c + SZ], 0.0)
            rows = pl.ds(SX * SZ * c + SZ * x, SZ)
            forces_rows[rows, 0, :] = force
            velocity_rows[rows, 0, :] = vel[c, x] + 0.5 * STEP * force
            places_rows[rows, 0, :] = jnp.where(live6, mine[c][:SZ], 0.0)
            for i, (src, dst) in enumerate(stores):
                pltpu.make_async_copy(src.at[rows], dst.at[rows], store_sem.at[i]).start()
        return 0

    lax.fori_loop(0, SX, one_row, 0)
    for i, (src, dst) in enumerate(stores):
        pltpu.make_async_copy(src, dst, store_sem.at[i]).wait()


def per_device(sizes, places, velocity, forces_old, counts, mig_atom, mig_face):
    shape = places.shape
    flat = (3, SX, SZ, CAP)
    lines = (3 * SX * SZ, 1, CAP)
    anywhere = pl.BlockSpec(memory_space=pltpu.HBM)
    vmem = pl.BlockSpec(memory_space=pltpu.VMEM)
    dma = pltpu.SemaphoreType.DMA
    halo = pl.pallas_call(
        functools.partial(exchange_kernel, sizes),
        out_shape=[
            jax.ShapeDtypeStruct((3, SX, 8, CAP), F32),
            jax.ShapeDtypeStruct(flat, F32),
            jax.ShapeDtypeStruct((2, 3, SX, 8, CAP), F32),
            jax.ShapeDtypeStruct((3, 2, 3, 8, CAP), F32),
            jax.ShapeDtypeStruct((3, 2, 2, 3, 8, CAP), F32),
        ],
        in_specs=[anywhere] * 6,
        out_specs=[vmem] * 5,
        scratch_shapes=[
            pltpu.SMEM(counts.shape, I32),
            pltpu.SMEM(mig_atom.shape, I32),
            pltpu.SMEM(mig_face.shape, I32),
            pltpu.VMEM(lines, F32),
            pltpu.VMEM(lines, F32),
            pltpu.VMEM(lines, F32),
            dma((6,)),
            pltpu.VMEM(flat, F32),
            pltpu.VMEM(flat, F32),
            pltpu.VMEM((8, CAP), F32),
            pltpu.VMEM((5, 8, CAP), F32),
            pltpu.VMEM((2, 3, 8, CAP), F32),
            dma((5,)), dma((5,)), dma((2,)), dma((2,)), dma((3, 2)), dma((3, 2)), dma((3, 2, 2)), dma((3, 2, 2)),
        ],
        compiler_params=pltpu.CompilerParams(collective_id=0, has_side_effects=True, vmem_limit_bytes=8 << 20),
        name="exchange",
    )(*[
        pltpu.with_memory_space_constraint(value, pltpu.HBM)
        for value in (
            counts, mig_atom, mig_face, places.reshape(lines), velocity.reshape(lines), forces_old.reshape(lines)
        )
    ])
    outs = pl.pallas_call(
        force_kernel,
        out_shape=[jax.ShapeDtypeStruct(lines, F32)] * 3,
        in_specs=[vmem] * 5,
        out_specs=[anywhere] * 3,
        scratch_shapes=[
            pltpu.VMEM((3, 3, 3, 8, 8, CAP), F32),
            pltpu.VMEM((NDIR, 4, 8, CAP), F32),
            pltpu.VMEM((NT, 3, 8, CAP), F32),
            pltpu.VMEM((CAP, CAP), F32),
            pltpu.VMEM((CAP, CAP), F32),
            pltpu.VMEM((3 * SZ, CAP, CAP), F32),
            pltpu.VMEM((3 * SZ, CAP, CAP), F32),
            pltpu.VMEM((2, 8, CAP), I32),
            pltpu.VMEM(lines, F32),
            pltpu.VMEM(lines, F32),
            pltpu.VMEM(lines, F32),
            dma((3,)),
        ],
        compiler_params=pltpu.CompilerParams(vmem_limit_bytes=16 << 20),
        name="forces",
    )(*halo)
    return tuple(out.reshape(shape) for out in outs)


def solution(mesh):
    sizes = tuple(mesh.shape[a] for a in ("gx", "gy", "gz"))
    block = P(None, "gx", "gy", "gz", None)
    moves = P("gx", "gy", "gz", None)
    return jax.shard_map(
        functools.partial(per_device, sizes),
        mesh=mesh,
        in_specs=(block, block, block, P("gx", "gy", "gz"), moves, moves),
        out_specs=(block, block, block),
        check_vma=False,
    )
```

```python
import functools

import jax
import jax.numpy as jnp
from jax import lax
from jax.experimental import pallas as pl
from jax.experimental.pallas import tpu as pltpu
from jax.sharding import PartitionSpec as P

MESH = pl.DeviceIdType.MESH
F32 = jnp.float32
I32 = jnp.int32
STEP = 0.005
RC = 2.5
SPACING = 1.1
EDGE = 24.0 * (2.0 * RC ** (-13) - RC ** (-7))
SIDE = (4.0 * SPACING, 4.0 * SPACING, SPACING * 8)
FAR = 1.0e4
REACH = RC * 1.0005
SX, SZ, CAP, MIG = 6, 6, 128, 16
NDIR = 27
ROWS = 4
NL = 2
NT = 32
PER = 3
SPLITS = tuple(range(16, CAP, 16))
EAGER = 4
GROUP = 8 * ROWS
BATCH = 6


def iota(shape, dim):
    return lax.broadcasted_iota(I32, shape, dim)


LANES = lax.GatherDimensionNumbers(
    offset_dims=(), collapsed_slice_dims=(1,), start_index_map=(1,), operand_batching_dims=(0,), start_indices_batching_dims=(0,)
)


def lane_gather(value, index):
    return lax.gather(
        value, index[..., None], LANES, slice_sizes=(1, 1), mode=lax.GatherScatterMode.PROMISE_IN_BOUNDS
    )


def exchange_kernel(sizes, counts_in, atoms_in, faces_in, places_in, velocity_in, forces_in,
                    own, vel, yblk, slab, zrow, splat,
                    counts, atoms, faces, places, velocity, forces, load_sem, drift, half, letter, inbox, zsend,
                    lsend, lrecv, bsend, brecv, ssend, srecv, zs, zr):
    n_gx, n_gy, n_gz = sizes
    me = (lax.axis_index("gx"), lax.axis_index("gy"), lax.axis_index("gz"))

    def at(dx, dy, dz):
        return (
            lax.rem(me[0] + dx + n_gx, n_gx),
            lax.rem(me[1] + dy + n_gy, n_gy),
            lax.rem(me[2] + dz + n_gz, n_gz),
        )

    barrier = pltpu.get_barrier_semaphore()
    around = [
        (dx, dy, dz) for dx in (0, 1) for dy in (-1, 0, 1) for dz in (-1, 0, 1) if (dx, dy, dz) != (0, 0, 0)
    ]
    for step in around:
        pl.semaphore_signal(barrier, inc=1, device_id=at(*step), device_id_type=MESH)

    loads = [
        pltpu.make_async_copy(src, dst, load_sem.at[i])
        for i, (src, dst) in enumerate((
            (places_in, places), (velocity_in, velocity), (forces_in, forces),
            (atoms_in, atoms), (faces_in, faces), (counts_in, counts),
        ))
    ]
    for load in loads:
        load.start()
    for load in loads:
        load.wait()
    for c in range(3):
        for x in range(SX):
            rows = slice(SZ * (SX * c + x), SZ * (SX * c + x) + SZ)
            h = velocity[rows, 0, :] + 0.5 * STEP * forces[rows, 0, :]
            half[c, x] = h
            drift[c, x] = places[rows, 0, :] + STEP * h

    sub8 = iota((8, CAP), 0)
    lane8 = iota((8, CAP), 1)
    lane1 = iota((1, CAP), 1)
    out_letter = jnp.where(sub8 == 6, -1.0, 0.0).astype(F32)
    leaving_cell = jnp.full((1, CAP), -1.0, F32)
    leaving_slot = jnp.full((1, CAP), -1.0, F32)
    for k in range(MIG):
        atom = atoms[0, 0, 0, k]
        face = faces[0, 0, 0, k]
        cell = lax.shift_right_logical(atom, 7)
        slot = atom & 127
        cx = lax.div(cell, SZ)
        cz = lax.rem(cell, SZ)
        axis = lax.shift_right_logical(face, 1)
        up = face & 1
        tile = jnp.zeros((8, CAP), F32)
        for c in range(6):
            source = drift if c < 3 else half
            row = source[c % 3, cx, pl.ds(cz, 1), :]
            tile = jnp.where(sub8 == c, jnp.broadcast_to(row, (8, CAP)), tile)
        column = jnp.sum(jnp.where(lane8 == slot, tile, 0.0), axis=1, keepdims=True)
        sign = (2 * up - 1).astype(F32)
        shift = jnp.where(axis == 2, SIDE[2], SIDE[0]).astype(F32) * sign
        sub_col = iota((8, 1), 0)
        column = column - jnp.where(sub_col == axis, shift, 0.0)
        nx = jnp.where(axis == 0, (1 - up) * (SX - 1), cx)
        nz = jnp.where(axis == 2, (1 - up) * (SZ - 1), cz)
        column = jnp.where(sub_col == 6, (nx * 8 + nz).astype(F32), column)
        out_letter = jnp.where(lane8 == 16 * (face ^ 1) + k, column, out_letter)
        leaving_cell = jnp.where(lane1 == 96 + k, (cx * 8 + cz).astype(F32), leaving_cell)
        leaving_slot = jnp.where(lane1 == 96 + k, slot.astype(F32), leaving_slot)
    letter[...] = out_letter

    pl.semaphore_wait(barrier, len(around))

    posts = []
    for box, step in enumerate(((1, 0, 0), (0, 1, 0), (0, -1, 0), (0, 0, 1), (0, 0, -1))):
        post = pltpu.make_async_remote_copy(
            src_ref=letter, dst_ref=inbox.at[box], send_sem=lsend.at[box], recv_sem=lrecv.at[box],
            device_id=at(*step), device_id_type=MESH,
        )
        post.start()
        posts.append(post)

    count_rows = []
    for x in range(SX):
        row = jnp.zeros((8, CAP), I32)
        for z in range(SZ):
            row = jnp.where(sub8 == z, counts[x, 0, z], row)
        count_rows.append(row)

    for post in posts:
        post.wait_recv()
    got = inbox[4]
    for box, top in ((3, 80), (2, 64), (1, 48), (0, 32)):
        got = jnp.where(lane8 < top, inbox[box], got)
    arriving_cell = jnp.where(lane1 < 96, got[6:7, :], -1.0)
    sub8f = sub8.astype(F32)
    here = []
    gone = []
    for x in range(SX):
        here.append((jnp.broadcast_to(arriving_cell, (8, CAP)) == sub8f + 8.0 * x).astype(F32))
        gone.append((jnp.broadcast_to(leaving_cell, (8, CAP)) == sub8f + 8.0 * x).astype(F32))
    here_all = jnp.concatenate(here, axis=0)
    gone_all = jnp.concatenate(gone, axis=0)
    earlier = (iota((CAP, CAP), 0) < iota((CAP, CAP), 1)).astype(jnp.bfloat16)
    rank = jnp.dot(here_all.astype(jnp.bfloat16), earlier, preferred_element_type=F32)
    slot_table = here_all * (rank + jnp.concatenate(count_rows, axis=0).astype(F32))
    target = jnp.sum(slot_table, axis=0, keepdims=True)
    target = jnp.where(lane1 < 96, target, leaving_slot)
    slot_hit = (jnp.broadcast_to(target, (CAP, CAP)) == iota((CAP, CAP), 0).astype(F32)).astype(jnp.bfloat16)
    pieces = [(here_all - gone_all).astype(jnp.bfloat16)]
    for c in range(6):
        part = here_all * jnp.broadcast_to(jnp.where(lane1 < 96, got[c : c + 1, :], 0.0), here_all.shape)
        for _ in range(3):
            top = part.astype(jnp.bfloat16)
            pieces.append(top)
            part = part - top.astype(F32)
    landed = lax.dot_general(
        jnp.concatenate(pieces, axis=0), slot_hit, (((1,), (1,)), ((), ())), preferred_element_type=F32
    )
    n = SX * 8

    def arrived(c, x):
        base = n * (1 + 3 * c) + 8 * x
        return (
            landed[base : base + SZ] + landed[base + n : base + n + SZ] + landed[base + 2 * n : base + 2 * n + SZ]
        )

    lane6 = iota((SZ, CAP), 1)
    for x in range(SX):
        delta = landed[8 * x : 8 * x + SZ]
        live = (lane6 < count_rows[x][:SZ]).astype(F32) + delta > 0.5
        came = delta > 0.5
        for c in range(3):
            place = jnp.where(came, arrived(c, x), drift[c, x])
            place = jnp.where(live, place, FAR)
            own[c, x, 0:SZ] = place
            own[c, x, SZ:8] = jnp.full((8 - SZ, CAP), FAR, F32)
            zsend[0, c, x : x + 1] = place[0:1]
            zsend[1, c, x : x + 1] = place[SZ - 1 : SZ]
            speed = jnp.where(came, arrived(3 + c, x), half[c, x])
            vel[c, x] = jnp.where(live, speed, 0.0)
    for side in range(2):
        for c in range(3):
            zsend[side, c, SX:8] = jnp.full((8 - SX, CAP), FAR, F32)

    copies = []

    def send(src, dst, ssem, rsem, step):
        copy = pltpu.make_async_remote_copy(
            src_ref=src, dst_ref=dst, send_sem=ssem, recv_sem=rsem, device_id=at(*step), device_id_type=MESH
        )
        copy.start()
        copies.append(copy)

    for dy in (1, -1, 0):
        there = 1 - dy
        for dx in (1, 0):
            for zi, dz in ((0, -1), (1, 1)):
                send(zsend.at[zi], zrow.at[there, dx, 1 - zi], zs.at[there, dx, zi], zr.at[there, dx, 1 - zi], (dx, dy, dz))
    for i, dy in enumerate((1, -1)):
        send(own.at[:, :, 0:SZ], yblk.at[i, :, :, 0:SZ], bsend.at[i], brecv.at[i], (0, dy, 0))
    for dy in (1, -1, 0):
        there = 1 - dy
        for s, x in ((0, 0), (1, SX - 1)):
            send(own.at[:, x, 0:SZ], slab.at[there, s, :, 0:SZ], ssend.at[there, s], srecv.at[there, s], (1, dy, 0))

    def spread(x, _):
        columns = jnp.concatenate([own[c, x] for c in range(3)] + [jnp.zeros((CAP - 24, CAP), F32)], axis=0).T
        for z in range(SZ):
            for c in range(3):
                splat[x, 3 * z + c] = jnp.broadcast_to(columns[:, 8 * c + z : 8 * c + z + 1], (CAP, CAP))
        return 0

    lax.fori_loop(0, SX, spread, 0)
    for post in posts:
        post.wait_send()
    for copy in copies:
        copy.wait_send()
    for i, dy in enumerate((1, -1)):
        pltpu.make_async_remote_copy(
            src_ref=own.at[:, :, 0:SZ], dst_ref=yblk.at[i, :, :, 0:SZ], send_sem=bsend.at[i], recv_sem=brecv.at[i],
            device_id=at(0, dy, 0), device_id_type=MESH).wait_recv()
    for y in range(3):
        for s in range(2):
            pltpu.make_async_remote_copy(
                src_ref=own.at[:, 0, 0:SZ], dst_ref=slab.at[y, s, :, 0:SZ], send_sem=ssend.at[y, s], recv_sem=srecv.at[y, s],
                device_id=at(1, 0, 0), device_id_type=MESH).wait_recv()
        for g in range(2):
            for s in range(2):
                pltpu.make_async_remote_copy(
                    src_ref=zsend.at[0], dst_ref=zrow.at[y, g, s], send_sem=zs.at[y, g, s], recv_sem=zr.at[y, g, s],
                    device_id=at(0, 0, 1), device_id_type=MESH).wait_recv()


def force_kernel(own, vel, yblk, slab, zrow, splat, out_places, out_velocity, out_forces,
                 near, packed, lists, reduced, sums_of, totals, where_to,
                 places_rows, velocity_rows, forces_rows, store_sem):
    sub8 = iota((8, CAP), 0)
    lane8 = iota((8, CAP), 1)

    for y in range(3):
        for c in range(3):
            for xi in range(8):
                if xi == 0:
                    tile = slab[y, 1, c]
                    low, high = (zrow[y, 1, s, c, SX - 1 : SX] for s in (0, 1))
                elif xi == 7:
                    tile = slab[y, 0, c]
                    low, high = (zrow[y, 1, s, c, 0:1] for s in (0, 1))
                else:
                    tile = own[c, xi - 1] if y == 1 else yblk[y // 2, c, xi - 1]
                    low, high = (zrow[y, 0, s, c, xi - 1 : xi] for s in (0, 1))
                below = jnp.where(sub8 == 0, jnp.broadcast_to(low, (8, CAP)), pltpu.roll(tile, 1, 0))
                above = jnp.where(sub8 == SZ - 1, jnp.broadcast_to(high, (8, CAP)), pltpu.roll(tile, 7, 0))
                for zi, value in enumerate((below, tile, above)):
                    if c == 1 and y != 1:
                        value = value + (y - 1) * SIDE[1]
                    if c == 2 and zi != 1:
                        value = value + (zi - 1) * SIDE[2]
                    near[zi, c, y, xi] = value

    prefix = (iota((CAP, CAP), 0) <= iota((CAP, CAP), 1)).astype(jnp.bfloat16)
    source = iota((CAP, CAP), 0)
    weights = jnp.concatenate(
        [prefix, jnp.ones((CAP, CAP), jnp.bfloat16)] + [(source < n).astype(jnp.bfloat16) for n in SPLITS], axis=1
    )
    lane6 = iota((SZ, CAP), 1)
    steps = [(0, 0, 0)] + [
        (dx, dy, dz) for dx in (-1, 0, 1) for dy in (-1, 0, 1) for dz in (-1, 0, 1) if (dx, dy, dz) != (0, 0, 0)
    ]

    stores = ((places_rows, out_places), (velocity_rows, out_velocity), (forces_rows, out_forces))

    def own_cells(x):
        mine = [near[1, c, 1, x + 1] for c in range(3)]
        return mine, mine[0] < 0.5 * FAR

    def build(x, packed):
        mine, live = own_cells(x)
        low = [jnp.broadcast_to(jnp.min(mine[c], axis=1, keepdims=True), (8, CAP)) for c in range(3)]
        high = [
            jnp.broadcast_to(jnp.max(jnp.where(live, mine[c], -FAR), axis=1, keepdims=True), (8, CAP))
            for c in range(3)
        ]

        def neighbour(step):
            dx, dy, dz = step
            value = [near[dz + 1, c, dy + 1, x + 1 + dx] for c in range(3)]
            if dx:
                value[0] = value[0] + dx * SIDE[0]
            return value

        masks = []
        for step in steps:
            value = neighbour(step)
            gaps = [value[c] - high[c] if s > 0 else low[c] - value[c] for c, s in enumerate(step) if s]
            if len(gaps) > 1:
                gaps = [jnp.maximum(gap, 0.0) for gap in gaps]
                hit = sum(gap * gap for gap in gaps) < REACH * REACH
            elif gaps:
                hit = gaps[0] < REACH
            if not any(s > 0 for s in step):
                alive = value[0] < 0.5 * FAR
                hit = hit & alive if gaps else alive
            masks.append(jnp.where(hit, 1.0, 0.0).astype(F32))
        ranks = jnp.dot(
            jnp.concatenate(masks, axis=0).astype(jnp.bfloat16), weights, preferred_element_type=F32
        )
        base = jnp.zeros((8, CAP), F32)
        for t in range(EAGER):
            for c in range(3):
                lists[x, t, c] = jnp.full((8, CAP), FAR, F32)
        wants = []
        windows = []
        at = []
        for d in range(NDIR):
            rank = [ranks[8 * d : 8 * d + 8, CAP * i : CAP * (i + 1)] for i in range(1, 2 + len(SPLITS))]
            base_int = base.astype(I32)
            want_int = (lane8 - base_int) & 127
            want = want_int.astype(F32)
            wants.append(want)
            windows.append(jnp.where(want < rank[0], lax.shift_right_logical(base_int + want_int, 7), -1))
            base = base + rank[0]
            passed = rank[1:]
            start = jnp.zeros((8, CAP), I32)
            width = CAP
            while passed:
                width //= 2
                half = len(passed) // 2
                over = passed[half] <= want
                start = jnp.where(over, start + width, start) if width < CAP // 2 else jnp.where(over, width, 0)
                passed = [jnp.where(over, b, a) for a, b in zip(passed[:half], passed[half + 1 :])]
            at.append(start + (width // 2 - 1))
        while width > 1:
            width //= 2
            step_by = width // 2
            for d in range(NDIR):
                seen = lane_gather(ranks[8 * d : 8 * d + 8, :CAP], at[d]) <= wants[d]
                at[d] = at[d] + jnp.where(seen, max(step_by, 1), -step_by)
        for d, step in enumerate(steps):
            value = neighbour(step)
            packed[d, 3] = windows[d].astype(F32)
            for c in range(3):
                chosen = lane_gather(value[c], at[d] & 127)
                packed[d, c] = chosen
                for t in range(EAGER):
                    pltpu.store(lists.at[x, t, c], chosen, mask=windows[d] == t)
        total = base.astype(I32)
        used = jnp.max(jnp.where(live, lane8 + 1, 0).astype(F32), axis=1, keepdims=True).astype(I32)
        list_steps = lax.shift_right_logical(total + (128 * NL - 1), 7 + (NL - 1))
        row_steps = lax.shift_right_logical(jnp.broadcast_to(used, (8, CAP)) + (8 * ROWS - 1), 3 + {1: 0, 2: 1, 4: 2, 8: 3}[ROWS])
        totals[x, 0] = list_steps
        totals[x, 1] = row_steps
        return jnp.max(jnp.where(sub8 < SZ, list_steps, 0))

    def build_rows(p, _):
        longest = [build(PER * p + i, packed.at[i]) for i in range(PER)]
        for i in range(PER):

            def fill(t, _):
                tf = t.astype(F32)
                got = [jnp.full((8, CAP), FAR, F32)] * 3
                for d in range(NDIR):
                    hit = packed[i, d, 3] == tf
                    got = [jnp.where(hit, packed[i, d, c], got[c]) for c in range(3)]
                for c in range(3):
                    lists[PER * p + i, t, c] = got[c]
                return 0

            lax.fori_loop(EAGER, longest[i] * NL, fill, 0)
        return 0

    lax.fori_loop(0, SX // PER, build_rows, 0)

    def one_row(x, n_done):
        for z in range(SZ):
            n_list = totals[x, 0, z, 0]
            n_rows = totals[x, 1, z, 0]

            def row_group(g, n_done):
                start = pl.multiple_of(g * GROUP, GROUP)

                def list_step(t, sums):
                    sums = list(sums)
                    for u in range(NL):
                        other = [
                            jnp.broadcast_to(lists[x, t * NL + u, c, z : z + 1, :], (8, CAP)) for c in range(3)
                        ]
                        for i in range(ROWS):
                            rows = pl.ds(pl.multiple_of(start + 8 * i, 8), 8)
                            delta = [splat[x, 3 * z + c, rows, :] - other[c] for c in range(3)]
                            square = delta[0] * delta[0] + delta[1] * delta[1] + delta[2] * delta[2]
                            root = lax.rsqrt(jnp.maximum(square, 0.01))
                            second = root * root
                            sixth = second * second * second
                            size = root * ((root * sixth) * (sixth - 0.5) - EDGE / 48.0)
                            size = jnp.where(square < RC * RC, size, 0.0)
                            for c in range(3):
                                sums[3 * i + c] = sums[3 * i + c] + delta[c] * size
                    return tuple(sums)

                sums = lax.fori_loop(
                    0, n_list, list_step, tuple(jnp.zeros((8, CAP), F32) for _ in range(3 * ROWS))
                )
                for i in range(3 * ROWS):
                    sums_of[n_done, i] = sums[i]
                where_to[0, n_done] = SZ * x + z
                where_to[1, n_done] = g
                return n_done + 1

            n_done = lax.fori_loop(0, n_rows, row_group, n_done)
        return n_done

    n_groups = lax.fori_loop(0, SX, one_row, 0)
    for i in range(BATCH):
        where_to[0, n_groups + i] = SX * SZ
        where_to[1, n_groups + i] = 0

    def sum_lanes(k, _):
        for j in range(BATCH):
            n = k * BATCH + j
            cell = where_to[0, n]
            start = where_to[1, n] * GROUP
            for i in range(ROWS):
                block = jnp.zeros((8, CAP), F32)
                for c in range(3):
                    total = jnp.sum(sums_of[n, 3 * i + c], axis=1, keepdims=True)
                    block = jnp.where(lax.shift_right_logical(lane8, 3) == c, total, block)
                reduced[cell, pl.ds(pl.multiple_of(start + 8 * i, 8), 8), :] = block
        return 0

    lax.fori_loop(0, lax.div(n_groups + (BATCH - 1), BATCH), sum_lanes, 0)

    for x in range(SX):
        mine, live = own_cells(x)
        lane = iota((CAP, CAP), 1) & 7
        columns = reduced[SZ * x]
        for z in range(1, SZ):
            columns = jnp.where(lane == z, reduced[SZ * x + z], columns)
        forces = columns.T
        for c in range(3):
            live6 = live[:SZ]
            force = jnp.where(live6, 48.0 * forces[8 * c : 8 * c + SZ], 0.0)
            rows = pl.ds(SX * SZ * c + SZ * x, SZ)
            forces_rows[rows, 0, :] = force
            velocity_rows[rows, 0, :] = vel[c, x] + 0.5 * STEP * force
            places_rows[rows, 0, :] = jnp.where(live6, mine[c][:SZ], 0.0)
            for i, (src, dst) in enumerate(stores):
                pltpu.make_async_copy(src.at[rows], dst.at[rows], store_sem.at[i]).start()
    for i, (src, dst) in enumerate(stores):
        pltpu.make_async_copy(src, dst, store_sem.at[i]).wait()


def per_device(sizes, places, velocity, forces_old, counts, mig_atom, mig_face):
    shape = places.shape
    flat = (3, SX, SZ, CAP)
    lines = (3 * SX * SZ, 1, CAP)
    anywhere = pl.BlockSpec(memory_space=pltpu.HBM)
    vmem = pl.BlockSpec(memory_space=pltpu.VMEM)
    dma = pltpu.SemaphoreType.DMA
    halo = pl.pallas_call(
        functools.partial(exchange_kernel, sizes),
        out_shape=[
            jax.ShapeDtypeStruct((3, SX, 8, CAP), F32),
            jax.ShapeDtypeStruct(flat, F32),
            jax.ShapeDtypeStruct((2, 3, SX, 8, CAP), F32),
            jax.ShapeDtypeStruct((3, 2, 3, 8, CAP), F32),
            jax.ShapeDtypeStruct((3, 2, 2, 3, 8, CAP), F32),
            jax.ShapeDtypeStruct((SX, 3 * SZ, CAP, CAP), F32),
        ],
        in_specs=[anywhere] * 6,
        out_specs=[vmem] * 6,
        scratch_shapes=[
            pltpu.SMEM(counts.shape, I32),
            pltpu.SMEM(mig_atom.shape, I32),
            pltpu.SMEM(mig_face.shape, I32),
            pltpu.VMEM(lines, F32),
            pltpu.VMEM(lines, F32),
            pltpu.VMEM(lines, F32),
            dma((6,)),
            pltpu.VMEM(flat, F32),
            pltpu.VMEM(flat, F32),
            pltpu.VMEM((8, CAP), F32),
            pltpu.VMEM((5, 8, CAP), F32),
            pltpu.VMEM((2, 3, 8, CAP), F32),
            dma((5,)), dma((5,)), dma((2,)), dma((2,)), dma((3, 2)), dma((3, 2)), dma((3, 2, 2)), dma((3, 2, 2)),
        ],
        compiler_params=pltpu.CompilerParams(collective_id=0, has_side_effects=True, vmem_limit_bytes=8 << 20),
        name="exchange",
    )(*[
        pltpu.with_memory_space_constraint(value, pltpu.HBM)
        for value in (
            counts, mig_atom, mig_face, places.reshape(lines), velocity.reshape(lines), forces_old.reshape(lines)
        )
    ])
    outs = pl.pallas_call(
        force_kernel,
        out_shape=[jax.ShapeDtypeStruct(lines, F32)] * 3,
        in_specs=[vmem] * 6,
        out_specs=[anywhere] * 3,
        scratch_shapes=[
            pltpu.VMEM((3, 3, 3, 8, 8, CAP), F32),
            pltpu.VMEM((PER, NDIR, 4, 8, CAP), F32),
            pltpu.VMEM((SX, NT, 3, 8, CAP), F32),
            pltpu.VMEM((SX * SZ + 1, CAP, CAP), F32),
            pltpu.VMEM((SX * SZ * (CAP // GROUP) + BATCH, 3 * ROWS, 8, CAP), F32),
            pltpu.VMEM((SX, 2, 8, CAP), I32),
            pltpu.SMEM((2, SX * SZ * (CAP // GROUP) + BATCH), I32),
            pltpu.VMEM(lines, F32),
            pltpu.VMEM(lines, F32),
            pltpu.VMEM(lines, F32),
            dma((3,)),
        ],
        compiler_params=pltpu.CompilerParams(vmem_limit_bytes=24 << 20),
        name="forces",
    )(*halo)
    return tuple(out.reshape(shape) for out in outs)


def solution(mesh):
    sizes = tuple(mesh.shape[a] for a in ("gx", "gy", "gz"))
    block = P(None, "gx", "gy", "gz", None)
    moves = P("gx", "gy", "gz", None)
    return jax.shard_map(
        functools.partial(per_device, sizes),
        mesh=mesh,
        in_specs=(block, block, block, P("gx", "gy", "gz"), moves, moves),
        out_specs=(block, block, block),
        check_vma=False,
    )
```

```python
import functools

import jax
import jax.numpy as jnp
from jax import lax
from jax.experimental import pallas as pl
from jax.experimental.pallas import tpu as pltpu
from jax.sharding import PartitionSpec as P

MESH = pl.DeviceIdType.MESH
F32 = jnp.float32
I32 = jnp.int32
STEP = 0.005
RC = 2.5
SPACING = 1.1
EDGE = 24.0 * (2.0 * RC ** (-13) - RC ** (-7))
SIDE = (4.0 * SPACING, 4.0 * SPACING, SPACING * 8)
FAR = 1.0e4
REACH = RC * 1.0005
SX, SZ, CAP, MIG = 6, 6, 128, 16
ROWS = 4
NL = 2
NT = 32
PER = 3
SPLITS = tuple(range(16, CAP, 16))
EAGER = 4
GROUP = 8 * ROWS
BATCH = 6


def iota(shape, dim):
    return lax.broadcasted_iota(I32, shape, dim)


LANES = lax.GatherDimensionNumbers(
    offset_dims=(), collapsed_slice_dims=(1,), start_index_map=(1,), operand_batching_dims=(0,), start_indices_batching_dims=(0,)
)


def lane_gather(value, index):
    return lax.gather(
        value, index[..., None], LANES, slice_sizes=(1, 1), mode=lax.GatherScatterMode.PROMISE_IN_BOUNDS
    )


STEPS = [(0, 0, 0)] + [
    (dx, dy, dz) for dx in (-1, 0, 1) for dy in (-1, 0, 1) for dz in (-1, 0, 1) if (dx, dy, dz) != (0, 0, 0)
]
LEVEL_STEPS = [step for step in STEPS if step[1] == 0]
OTHER_STEPS = [step for step in STEPS if step[1] != 0]


def three_layers(tile, low, high, c, dy):
    rows = iota((8, CAP), 0)
    below = jnp.where(rows == 0, jnp.broadcast_to(low, (8, CAP)), pltpu.roll(tile, 1, 0))
    above = jnp.where(rows == SZ - 1, jnp.broadcast_to(high, (8, CAP)), pltpu.roll(tile, 7, 0))
    values = [below, tile, above]
    if c == 1 and dy:
        values = [value + dy * SIDE[1] for value in values]
    if c == 2:
        values = [value + dz * SIDE[2] if dz else value for dz, value in zip((-1, 0, 1), values)]
    return values


def box_of(mine):
    live = mine[0] < 0.5 * FAR
    low = [jnp.broadcast_to(jnp.min(mine[c], axis=1, keepdims=True), (8, CAP)) for c in range(3)]
    high = [
        jnp.broadcast_to(jnp.max(jnp.where(live, mine[c], -FAR), axis=1, keepdims=True), (8, CAP)) for c in range(3)
    ]
    return low, high


def rank_weights():
    source, target = iota((CAP, CAP), 0), iota((CAP, CAP), 1)
    return jnp.concatenate(
        [(source <= target).astype(jnp.bfloat16), jnp.ones((CAP, CAP), jnp.bfloat16)]
        + [(source < n).astype(jnp.bfloat16) for n in SPLITS],
        axis=1,
    )


def search(steps, neighbour, box, base, weights, emit):
    lane8 = iota((8, CAP), 1)
    low, high = box
    masks = []
    for step in steps:
        value = neighbour(step)
        gaps = [value[c] - high[c] if s > 0 else low[c] - value[c] for c, s in enumerate(step) if s]
        if len(gaps) > 1:
            gaps = [jnp.maximum(gap, 0.0) for gap in gaps]
            hit = sum(gap * gap for gap in gaps) < REACH * REACH
        elif gaps:
            hit = gaps[0] < REACH
        if not any(s > 0 for s in step):
            alive = value[0] < 0.5 * FAR
            hit = hit & alive if gaps else alive
        masks.append(jnp.where(hit, 1.0, 0.0).astype(F32))
    ranks = jnp.dot(
        jnp.concatenate(masks, axis=0).astype(jnp.bfloat16), weights, preferred_element_type=F32
    )
    wants = []
    windows = []
    at = []
    for d in range(len(steps)):
        rank = [ranks[8 * d : 8 * d + 8, CAP * i : CAP * (i + 1)] for i in range(1, 2 + len(SPLITS))]
        base_int = base.astype(I32)
        want_int = (lane8 - base_int) & 127
        want = want_int.astype(F32)
        wants.append(want)
        windows.append(jnp.where(want < rank[0], lax.shift_right_logical(base_int + want_int, 7), -1))
        base = base + rank[0]
        passed = rank[1:]
        start = jnp.zeros((8, CAP), I32)
        width = CAP
        while passed:
            width //= 2
            half = len(passed) // 2
            over = passed[half] <= want
            start = jnp.where(over, start + width, start) if width < CAP // 2 else jnp.where(over, width, 0)
            passed = [jnp.where(over, b, a) for a, b in zip(passed[:half], passed[half + 1 :])]
        at.append(start + (width // 2 - 1))
    while width > 1:
        width //= 2
        step_by = width // 2
        for d in range(len(steps)):
            seen = lane_gather(ranks[8 * d : 8 * d + 8, :CAP], at[d]) <= wants[d]
            at[d] = at[d] + jnp.where(seen, max(step_by, 1), -step_by)
    for d, step in enumerate(steps):
        value = neighbour(step)
        emit(d, windows[d].astype(F32), [lane_gather(value[c], at[d] & 127) for c in range(3)])
    return base


def exchange_kernel(sizes, counts_in, atoms_in, faces_in, places_in, velocity_in, forces_in,
                    own, vel, yblk, slab, zrow, splat, level, level_packed, level_base,
                    counts, atoms, faces, places, velocity, forces, load_sem, drift, half, letter, inbox, zsend,
                    lsend, lrecv, bsend, brecv, ssend, srecv, zs, zr):
    n_gx, n_gy, n_gz = sizes
    me = (lax.axis_index("gx"), lax.axis_index("gy"), lax.axis_index("gz"))

    def at(dx, dy, dz):
        return (
            lax.rem(me[0] + dx + n_gx, n_gx),
            lax.rem(me[1] + dy + n_gy, n_gy),
            lax.rem(me[2] + dz + n_gz, n_gz),
        )

    barrier = pltpu.get_barrier_semaphore()
    around = [
        (dx, dy, dz) for dx in (0, 1) for dy in (-1, 0, 1) for dz in (-1, 0, 1) if (dx, dy, dz) != (0, 0, 0)
    ]
    for step in around:
        pl.semaphore_signal(barrier, inc=1, device_id=at(*step), device_id_type=MESH)

    loads = [
        pltpu.make_async_copy(src, dst, load_sem.at[i])
        for i, (src, dst) in enumerate((
            (places_in, places), (velocity_in, velocity), (forces_in, forces),
            (atoms_in, atoms), (faces_in, faces), (counts_in, counts),
        ))
    ]
    for load in loads:
        load.start()
    for load in loads:
        load.wait()
    for c in range(3):
        for x in range(SX):
            rows = slice(SZ * (SX * c + x), SZ * (SX * c + x) + SZ)
            h = velocity[rows, 0, :] + 0.5 * STEP * forces[rows, 0, :]
            half[c, x] = h
            drift[c, x] = places[rows, 0, :] + STEP * h

    sub8 = iota((8, CAP), 0)
    lane8 = iota((8, CAP), 1)
    lane1 = iota((1, CAP), 1)
    out_letter = jnp.where(sub8 == 6, -1.0, 0.0).astype(F32)
    leaving_cell = jnp.full((1, CAP), -1.0, F32)
    leaving_slot = jnp.full((1, CAP), -1.0, F32)
    for k in range(MIG):
        atom = atoms[0, 0, 0, k]
        face = faces[0, 0, 0, k]
        cell = lax.shift_right_logical(atom, 7)
        slot = atom & 127
        cx = lax.div(cell, SZ)
        cz = lax.rem(cell, SZ)
        axis = lax.shift_right_logical(face, 1)
        up = face & 1
        tile = jnp.zeros((8, CAP), F32)
        for c in range(6):
            source = drift if c < 3 else half
            row = source[c % 3, cx, pl.ds(cz, 1), :]
            tile = jnp.where(sub8 == c, jnp.broadcast_to(row, (8, CAP)), tile)
        column = jnp.sum(jnp.where(lane8 == slot, tile, 0.0), axis=1, keepdims=True)
        sign = (2 * up - 1).astype(F32)
        shift = jnp.where(axis == 2, SIDE[2], SIDE[0]).astype(F32) * sign
        sub_col = iota((8, 1), 0)
        column = column - jnp.where(sub_col == axis, shift, 0.0)
        nx = jnp.where(axis == 0, (1 - up) * (SX - 1), cx)
        nz = jnp.where(axis == 2, (1 - up) * (SZ - 1), cz)
        column = jnp.where(sub_col == 6, (nx * 8 + nz).astype(F32), column)
        out_letter = jnp.where(lane8 == 16 * (face ^ 1) + k, column, out_letter)
        leaving_cell = jnp.where(lane1 == 96 + k, (cx * 8 + cz).astype(F32), leaving_cell)
        leaving_slot = jnp.where(lane1 == 96 + k, slot.astype(F32), leaving_slot)
    letter[...] = out_letter

    pl.semaphore_wait(barrier, len(around))

    posts = []
    for box, step in enumerate(((1, 0, 0), (0, 1, 0), (0, -1, 0), (0, 0, 1), (0, 0, -1))):
        post = pltpu.make_async_remote_copy(
            src_ref=letter, dst_ref=inbox.at[box], send_sem=lsend.at[box], recv_sem=lrecv.at[box],
            device_id=at(*step), device_id_type=MESH,
        )
        post.start()
        posts.append(post)

    count_rows = []
    for x in range(SX):
        row = jnp.zeros((8, CAP), I32)
        for z in range(SZ):
            row = jnp.where(sub8 == z, counts[x, 0, z], row)
        count_rows.append(row)

    for post in posts:
        post.wait_recv()
    got = inbox[4]
    for box, top in ((3, 80), (2, 64), (1, 48), (0, 32)):
        got = jnp.where(lane8 < top, inbox[box], got)
    arriving_cell = jnp.where(lane1 < 96, got[6:7, :], -1.0)
    sub8f = sub8.astype(F32)
    here = []
    gone = []
    for x in range(SX):
        here.append((jnp.broadcast_to(arriving_cell, (8, CAP)) == sub8f + 8.0 * x).astype(F32))
        gone.append((jnp.broadcast_to(leaving_cell, (8, CAP)) == sub8f + 8.0 * x).astype(F32))
    here_all = jnp.concatenate(here, axis=0)
    gone_all = jnp.concatenate(gone, axis=0)
    earlier = (iota((CAP, CAP), 0) < iota((CAP, CAP), 1)).astype(jnp.bfloat16)
    rank = jnp.dot(here_all.astype(jnp.bfloat16), earlier, preferred_element_type=F32)
    slot_table = here_all * (rank + jnp.concatenate(count_rows, axis=0).astype(F32))
    target = jnp.sum(slot_table, axis=0, keepdims=True)
    target = jnp.where(lane1 < 96, target, leaving_slot)
    slot_hit = (jnp.broadcast_to(target, (CAP, CAP)) == iota((CAP, CAP), 0).astype(F32)).astype(jnp.bfloat16)
    pieces = [(here_all - gone_all).astype(jnp.bfloat16)]
    for c in range(6):
        part = here_all * jnp.broadcast_to(jnp.where(lane1 < 96, got[c : c + 1, :], 0.0), here_all.shape)
        for _ in range(3):
            top = part.astype(jnp.bfloat16)
            pieces.append(top)
            part = part - top.astype(F32)
    landed = lax.dot_general(
        jnp.concatenate(pieces, axis=0), slot_hit, (((1,), (1,)), ((), ())), preferred_element_type=F32
    )
    n = SX * 8

    def arrived(c, x):
        base = n * (1 + 3 * c) + 8 * x
        return (
            landed[base : base + SZ] + landed[base + n : base + n + SZ] + landed[base + 2 * n : base + 2 * n + SZ]
        )

    lane6 = iota((SZ, CAP), 1)
    for x in range(SX):
        delta = landed[8 * x : 8 * x + SZ]
        live = (lane6 < count_rows[x][:SZ]).astype(F32) + delta > 0.5
        came = delta > 0.5
        for c in range(3):
            place = jnp.where(came, arrived(c, x), drift[c, x])
            place = jnp.where(live, place, FAR)
            own[c, x, 0:SZ] = place
            own[c, x, SZ:8] = jnp.full((8 - SZ, CAP), FAR, F32)
            zsend[0, c, x : x + 1] = place[0:1]
            zsend[1, c, x : x + 1] = place[SZ - 1 : SZ]
            speed = jnp.where(came, arrived(3 + c, x), half[c, x])
            vel[c, x] = jnp.where(live, speed, 0.0)
    for side in range(2):
        for c in range(3):
            zsend[side, c, SX:8] = jnp.full((8 - SX, CAP), FAR, F32)

    copies = []

    def send(src, dst, ssem, rsem, step):
        copy = pltpu.make_async_remote_copy(
            src_ref=src, dst_ref=dst, send_sem=ssem, recv_sem=rsem, device_id=at(*step), device_id_type=MESH
        )
        copy.start()
        copies.append(copy)

    for dy in (1, -1, 0):
        there = 1 - dy
        for dx in (1, 0):
            for zi, dz in ((0, -1), (1, 1)):
                send(zsend.at[zi], zrow.at[there, dx, 1 - zi], zs.at[there, dx, zi], zr.at[there, dx, 1 - zi], (dx, dy, dz))
    for i, dy in enumerate((1, -1)):
        send(own.at[:, :, 0:SZ], yblk.at[i, :, :, 0:SZ], bsend.at[i], brecv.at[i], (0, dy, 0))
    for dy in (1, -1, 0):
        there = 1 - dy
        for s, x in ((0, 0), (1, SX - 1)):
            send(own.at[:, x, 0:SZ], slab.at[there, s, :, 0:SZ], ssend.at[there, s], srecv.at[there, s], (1, dy, 0))

    def spread(x, _):
        columns = jnp.concatenate([own[c, x] for c in range(3)] + [jnp.zeros((CAP - 24, CAP), F32)], axis=0).T
        for z in range(SZ):
            for c in range(3):
                splat[x, 3 * z + c] = jnp.broadcast_to(columns[:, 8 * c + z : 8 * c + z + 1], (CAP, CAP))
        return 0

    lax.fori_loop(0, SX, spread, 0)

    def arrived_slab(y, side):
        pltpu.make_async_remote_copy(
            src_ref=own.at[:, 0, 0:SZ], dst_ref=slab.at[y, side, :, 0:SZ], send_sem=ssend.at[y, side],
            recv_sem=srecv.at[y, side], device_id=at(1, 0, 0), device_id_type=MESH,
        ).wait_recv()

    def arrived_row(y, g, side):
        pltpu.make_async_remote_copy(
            src_ref=zsend.at[0], dst_ref=zrow.at[y, g, side], send_sem=zs.at[y, g, side],
            recv_sem=zr.at[y, g, side], device_id=at(0, 0, 1), device_id_type=MESH,
        ).wait_recv()

    for side in range(2):
        arrived_slab(1, side)
        for g in range(2):
            arrived_row(1, g, side)

    for c in range(3):
        for xi in range(8):
            if 0 < xi < 7:
                tile = own[c, xi - 1]
                edges = [zrow[1, 0, side, c, xi - 1 : xi] for side in (0, 1)]
            else:
                cell = SX - 1 if xi == 0 else 0
                tile = jnp.concatenate(
                    [slab[1, 1 if xi == 0 else 0, c, 0:SZ], jnp.full((8 - SZ, CAP), FAR, F32)], axis=0
                )
                edges = [zrow[1, 1, side, c, cell : cell + 1] for side in (0, 1)]
            for zi, value in enumerate(three_layers(tile, *edges, c, 0)):
                level[zi, c, xi] = value
    weights = rank_weights()

    def level_rows(p, _):
        for i in range(PER):
            x = PER * p + i

            def neighbour(step):
                value = [level[step[2] + 1, c, x + 1 + step[0]] for c in range(3)]
                if step[0]:
                    value[0] = value[0] + step[0] * SIDE[0]
                return value

            def emit(d, window, chosen):
                level_packed[x, d, 3] = window
                for c in range(3):
                    level_packed[x, d, c] = chosen[c]

            level_base[x] = search(
                LEVEL_STEPS, neighbour, box_of(neighbour((0, 0, 0))), jnp.zeros((8, CAP), F32), weights, emit
            )
        return 0

    lax.fori_loop(0, SX // PER, level_rows, 0)

    for post in posts:
        post.wait_send()
    for copy in copies:
        copy.wait_send()
    for i, dy in enumerate((1, -1)):
        pltpu.make_async_remote_copy(
            src_ref=own.at[:, :, 0:SZ], dst_ref=yblk.at[i, :, :, 0:SZ], send_sem=bsend.at[i], recv_sem=brecv.at[i],
            device_id=at(0, dy, 0), device_id_type=MESH).wait_recv()
    for y in (0, 2):
        for side in range(2):
            arrived_slab(y, side)
            for g in range(2):
                arrived_row(y, g, side)


def force_kernel(own, vel, yblk, slab, zrow, splat, level, level_packed, level_base, out_places, out_velocity, out_forces,
                 near, packed, lists, reduced, sums_of, totals, where_to,
                 places_rows, velocity_rows, forces_rows, store_sem):
    sub8 = iota((8, CAP), 0)
    lane8 = iota((8, CAP), 1)

    for side, y in ((0, 0), (1, 2)):
        for c in range(3):
            for xi in range(8):
                if xi == 0:
                    tile = slab[y, 1, c]
                    edges = [zrow[y, 1, s, c, SX - 1 : SX] for s in (0, 1)]
                elif xi == 7:
                    tile = slab[y, 0, c]
                    edges = [zrow[y, 1, s, c, 0:1] for s in (0, 1)]
                else:
                    tile = yblk[side, c, xi - 1]
                    edges = [zrow[y, 0, s, c, xi - 1 : xi] for s in (0, 1)]
                for zi, value in enumerate(three_layers(tile, *edges, c, y - 1)):
                    near[zi, c, side, xi] = value

    weights = rank_weights()
    stores = ((places_rows, out_places), (velocity_rows, out_velocity), (forces_rows, out_forces))

    def own_cells(x):
        mine = [level[1, c, x + 1] for c in range(3)]
        return mine, mine[0] < 0.5 * FAR

    def build(x, packed):
        mine, live = own_cells(x)

        def neighbour(step):
            dx, dy, dz = step
            value = [near[dz + 1, c, (dy + 1) // 2, x + 1 + dx] for c in range(3)]
            if dx:
                value[0] = value[0] + dx * SIDE[0]
            return value

        for t in range(EAGER):
            for c in range(3):
                lists[x, t, c] = jnp.full((8, CAP), FAR, F32)

        def place(window, chosen):
            for t in range(EAGER):
                for c in range(3):
                    pltpu.store(lists.at[x, t, c], chosen[c], mask=window == float(t))

        def emit(d, window, chosen):
            packed[d, 3] = window
            for c in range(3):
                packed[d, c] = chosen[c]
            place(window, chosen)

        for d in range(len(LEVEL_STEPS)):
            place(level_packed[x, d, 3], [level_packed[x, d, c] for c in range(3)])
        base = search(OTHER_STEPS, neighbour, box_of(mine), level_base[x], weights, emit)
        total = base.astype(I32)
        used = jnp.max(jnp.where(live, lane8 + 1, 0).astype(F32), axis=1, keepdims=True).astype(I32)
        list_steps = lax.shift_right_logical(total + (128 * NL - 1), 7 + (NL - 1))
        row_steps = lax.shift_right_logical(jnp.broadcast_to(used, (8, CAP)) + (8 * ROWS - 1), 3 + {1: 0, 2: 1, 4: 2, 8: 3}[ROWS])
        totals[x, 0] = list_steps
        totals[x, 1] = row_steps
        return jnp.max(jnp.where(sub8 < SZ, list_steps, 0))

    def build_rows(p, _):
        longest = [build(PER * p + i, packed.at[i]) for i in range(PER)]
        for i in range(PER):

            def fill(t, _):
                tf = t.astype(F32)
                got = [jnp.full((8, CAP), FAR, F32)] * 3
                for source in [level_packed.at[PER * p + i, d] for d in range(len(LEVEL_STEPS))] + [
                    packed.at[i, d] for d in range(len(OTHER_STEPS))
                ]:
                    hit = source[3] == tf
                    got = [jnp.where(hit, source[c], got[c]) for c in range(3)]
                for c in range(3):
                    lists[PER * p + i, t, c] = got[c]
                return 0

            lax.fori_loop(EAGER, longest[i] * NL, fill, 0)
        return 0

    lax.fori_loop(0, SX // PER, build_rows, 0)

    def one_row(x, n_done):
        for z in range(SZ):
            n_list = totals[x, 0, z, 0]
            n_rows = totals[x, 1, z, 0]

            def row_group(g, n_done):
                start = pl.multiple_of(g * GROUP, GROUP)

                def list_step(t, sums):
                    sums = list(sums)
                    for u in range(NL):
                        other = [
                            jnp.broadcast_to(lists[x, t * NL + u, c, z : z + 1, :], (8, CAP)) for c in range(3)
                        ]
                        for i in range(ROWS):
                            rows = pl.ds(pl.multiple_of(start + 8 * i, 8), 8)
                            delta = [splat[x, 3 * z + c, rows, :] - other[c] for c in range(3)]
                            square = delta[0] * delta[0] + delta[1] * delta[1] + delta[2] * delta[2]
                            root = lax.rsqrt(jnp.maximum(square, 0.01))
                            second = root * root
                            sixth = second * second * second
                            size = root * ((root * sixth) * (sixth - 0.5) - EDGE / 48.0)
                            size = jnp.where(square < RC * RC, size, 0.0)
                            for c in range(3):
                                sums[3 * i + c] = sums[3 * i + c] + delta[c] * size
                    return tuple(sums)

                sums = lax.fori_loop(
                    0, n_list, list_step, tuple(jnp.zeros((8, CAP), F32) for _ in range(3 * ROWS))
                )
                for i in range(3 * ROWS):
                    sums_of[n_done, i] = sums[i]
                where_to[0, n_done] = SZ * x + z
                where_to[1, n_done] = g
                return n_done + 1

            n_done = lax.fori_loop(0, n_rows, row_group, n_done)
        return n_done

    n_groups = lax.fori_loop(0, SX, one_row, 0)
    for i in range(BATCH):
        where_to[0, n_groups + i] = SX * SZ
        where_to[1, n_groups + i] = 0

    def sum_lanes(k, _):
        for j in range(BATCH):
            n = k * BATCH + j
            cell = where_to[0, n]
            start = where_to[1, n] * GROUP
            for i in range(ROWS):
                block = jnp.zeros((8, CAP), F32)
                for c in range(3):
                    total = jnp.sum(sums_of[n, 3 * i + c], axis=1, keepdims=True)
                    block = jnp.where(lax.shift_right_logical(lane8, 3) == c, total, block)
                reduced[cell, pl.ds(pl.multiple_of(start + 8 * i, 8), 8), :] = block
        return 0

    lax.fori_loop(0, lax.div(n_groups + (BATCH - 1), BATCH), sum_lanes, 0)

    for x in range(SX):
        mine, live = own_cells(x)
        lane = iota((CAP, CAP), 1) & 7
        columns = reduced[SZ * x]
        for z in range(1, SZ):
            columns = jnp.where(lane == z, reduced[SZ * x + z], columns)
        forces = columns.T
        for c in range(3):
            live6 = live[:SZ]
            force = jnp.where(live6, 48.0 * forces[8 * c : 8 * c + SZ], 0.0)
            rows = pl.ds(SX * SZ * c + SZ * x, SZ)
            forces_rows[rows, 0, :] = force
            velocity_rows[rows, 0, :] = vel[c, x] + 0.5 * STEP * force
            places_rows[rows, 0, :] = jnp.where(live6, mine[c][:SZ], 0.0)
            for i, (src, dst) in enumerate(stores):
                pltpu.make_async_copy(src.at[rows], dst.at[rows], store_sem.at[i]).start()
    for i, (src, dst) in enumerate(stores):
        pltpu.make_async_copy(src, dst, store_sem.at[i]).wait()


def per_device(sizes, places, velocity, forces_old, counts, mig_atom, mig_face):
    shape = places.shape
    flat = (3, SX, SZ, CAP)
    lines = (3 * SX * SZ, 1, CAP)
    anywhere = pl.BlockSpec(memory_space=pltpu.HBM)
    vmem = pl.BlockSpec(memory_space=pltpu.VMEM)
    dma = pltpu.SemaphoreType.DMA
    halo = pl.pallas_call(
        functools.partial(exchange_kernel, sizes),
        out_shape=[
            jax.ShapeDtypeStruct((3, SX, 8, CAP), F32),
            jax.ShapeDtypeStruct(flat, F32),
            jax.ShapeDtypeStruct((2, 3, SX, 8, CAP), F32),
            jax.ShapeDtypeStruct((3, 2, 3, 8, CAP), F32),
            jax.ShapeDtypeStruct((3, 2, 2, 3, 8, CAP), F32),
            jax.ShapeDtypeStruct((SX, 3 * SZ, CAP, CAP), F32),
            jax.ShapeDtypeStruct((3, 3, 8, 8, CAP), F32),
            jax.ShapeDtypeStruct((SX, len(LEVEL_STEPS), 4, 8, CAP), F32),
            jax.ShapeDtypeStruct((SX, 8, CAP), F32),
        ],
        in_specs=[anywhere] * 6,
        out_specs=[vmem] * 9,
        scratch_shapes=[
            pltpu.SMEM(counts.shape, I32),
            pltpu.SMEM(mig_atom.shape, I32),
            pltpu.SMEM(mig_face.shape, I32),
            pltpu.VMEM(lines, F32),
            pltpu.VMEM(lines, F32),
            pltpu.VMEM(lines, F32),
            dma((6,)),
            pltpu.VMEM(flat, F32),
            pltpu.VMEM(flat, F32),
            pltpu.VMEM((8, CAP), F32),
            pltpu.VMEM((5, 8, CAP), F32),
            pltpu.VMEM((2, 3, 8, CAP), F32),
            dma((5,)), dma((5,)), dma((2,)), dma((2,)), dma((3, 2)), dma((3, 2)), dma((3, 2, 2)), dma((3, 2, 2)),
        ],
        compiler_params=pltpu.CompilerParams(collective_id=0, has_side_effects=True, vmem_limit_bytes=8 << 20),
        name="exchange",
    )(*[
        pltpu.with_memory_space_constraint(value, pltpu.HBM)
        for value in (
            counts, mig_atom, mig_face, places.reshape(lines), velocity.reshape(lines), forces_old.reshape(lines)
        )
    ])
    outs = pl.pallas_call(
        force_kernel,
        out_shape=[jax.ShapeDtypeStruct(lines, F32)] * 3,
        in_specs=[vmem] * 9,
        out_specs=[anywhere] * 3,
        scratch_shapes=[
            pltpu.VMEM((3, 3, 2, 8, 8, CAP), F32),
            pltpu.VMEM((PER, len(OTHER_STEPS), 4, 8, CAP), F32),
            pltpu.VMEM((SX, NT, 3, 8, CAP), F32),
            pltpu.VMEM((SX * SZ + 1, CAP, CAP), F32),
            pltpu.VMEM((SX * SZ * (CAP // GROUP) + BATCH, 3 * ROWS, 8, CAP), F32),
            pltpu.VMEM((SX, 2, 8, CAP), I32),
            pltpu.SMEM((2, SX * SZ * (CAP // GROUP) + BATCH), I32),
            pltpu.VMEM(lines, F32),
            pltpu.VMEM(lines, F32),
            pltpu.VMEM(lines, F32),
            dma((3,)),
        ],
        compiler_params=pltpu.CompilerParams(vmem_limit_bytes=24 << 20),
        name="forces",
    )(*halo)
    return tuple(out.reshape(shape) for out in outs)


def solution(mesh):
    sizes = tuple(mesh.shape[a] for a in ("gx", "gy", "gz"))
    block = P(None, "gx", "gy", "gz", None)
    moves = P("gx", "gy", "gz", None)
    return jax.shard_map(
        functools.partial(per_device, sizes),
        mesh=mesh,
        in_specs=(block, block, block, P("gx", "gy", "gz"), moves, moves),
        out_specs=(block, block, block),
        check_vma=False,
    )
```

```python
import functools

import jax
import jax.numpy as jnp
from jax import lax
from jax.experimental import pallas as pl
from jax.experimental.pallas import tpu as pltpu
from jax.sharding import PartitionSpec as P

MESH = pl.DeviceIdType.MESH
F32 = jnp.float32
I32 = jnp.int32
STEP = 0.005
RC = 2.5
SPACING = 1.1
EDGE = 24.0 * (2.0 * RC ** (-13) - RC ** (-7))
SIDE = (4.0 * SPACING, 4.0 * SPACING, SPACING * 8)
FAR = 1.0e4
REACH = RC * 1.0005
SX, SZ, CAP, MIG = 6, 6, 128, 16
ROWS = 4
NL = 2
NT = 32
PER = 3
SPLITS = tuple(range(16, CAP, 16))
EAGER = 4
GROUP = 8 * ROWS
BATCH = 12


def iota(shape, dim):
    return lax.broadcasted_iota(I32, shape, dim)


LANES = lax.GatherDimensionNumbers(
    offset_dims=(), collapsed_slice_dims=(1,), start_index_map=(1,), operand_batching_dims=(0,), start_indices_batching_dims=(0,)
)


def lane_gather(value, index):
    return lax.gather(
        value, index[..., None], LANES, slice_sizes=(1, 1), mode=lax.GatherScatterMode.PROMISE_IN_BOUNDS
    )


STEPS = [(0, 0, 0)] + [
    (dx, dy, dz) for dx in (-1, 0, 1) for dy in (-1, 0, 1) for dz in (-1, 0, 1) if (dx, dy, dz) != (0, 0, 0)
]
LEVEL_STEPS = [step for step in STEPS if step[1] == 0]
OTHER_STEPS = [step for step in STEPS if step[1] != 0]


def three_layers(tile, low, high, c, dy):
    rows = iota((8, CAP), 0)
    below = jnp.where(rows == 0, jnp.broadcast_to(low, (8, CAP)), pltpu.roll(tile, 1, 0))
    above = jnp.where(rows == SZ - 1, jnp.broadcast_to(high, (8, CAP)), pltpu.roll(tile, 7, 0))
    values = [below, tile, above]
    if c == 1 and dy:
        values = [value + dy * SIDE[1] for value in values]
    if c == 2:
        values = [value + dz * SIDE[2] if dz else value for dz, value in zip((-1, 0, 1), values)]
    return values


def box_of(mine):
    live = mine[0] < 0.5 * FAR
    low = [jnp.broadcast_to(jnp.min(mine[c], axis=1, keepdims=True), (8, CAP)) for c in range(3)]
    high = [
        jnp.broadcast_to(jnp.max(jnp.where(live, mine[c], -FAR), axis=1, keepdims=True), (8, CAP)) for c in range(3)
    ]
    return low, high


def rank_weights():
    source, target = iota((CAP, CAP), 0), iota((CAP, CAP), 1)
    return jnp.concatenate(
        [(source <= target).astype(jnp.bfloat16), jnp.ones((CAP, CAP), jnp.bfloat16)]
        + [(source < n).astype(jnp.bfloat16) for n in SPLITS],
        axis=1,
    )


def search(steps, neighbour, box, base, weights, emit):
    lane8 = iota((8, CAP), 1)
    low, high = box
    masks = []
    for step in steps:
        value = neighbour(step)
        gaps = [value[c] - high[c] if s > 0 else low[c] - value[c] for c, s in enumerate(step) if s]
        if len(gaps) > 1:
            gaps = [jnp.maximum(gap, 0.0) for gap in gaps]
            hit = sum(gap * gap for gap in gaps) < REACH * REACH
        elif gaps:
            hit = gaps[0] < REACH
        if not any(s > 0 for s in step):
            alive = value[0] < 0.5 * FAR
            hit = hit & alive if gaps else alive
        masks.append(jnp.where(hit, 1.0, 0.0).astype(F32))
    ranks = jnp.dot(
        jnp.concatenate(masks, axis=0).astype(jnp.bfloat16), weights, preferred_element_type=F32
    )
    wants = []
    windows = []
    at = []
    for d in range(len(steps)):
        rank = [ranks[8 * d : 8 * d + 8, CAP * i : CAP * (i + 1)] for i in range(1, 2 + len(SPLITS))]
        base_int = base.astype(I32)
        want_int = (lane8 - base_int) & 127
        want = want_int.astype(F32)
        wants.append(want)
        windows.append(jnp.where(want < rank[0], lax.shift_right_logical(base_int + want_int, 7), -1))
        base = base + rank[0]
        passed = rank[1:]
        start = jnp.zeros((8, CAP), I32)
        width = CAP
        while passed:
            width //= 2
            half = len(passed) // 2
            over = passed[half] <= want
            start = jnp.where(over, start + width, start) if width < CAP // 2 else jnp.where(over, width, 0)
            passed = [jnp.where(over, b, a) for a, b in zip(passed[:half], passed[half + 1 :])]
        at.append(start + (width // 2 - 1))
    while width > 1:
        width //= 2
        step_by = width // 2
        for d in range(len(steps)):
            seen = lane_gather(ranks[8 * d : 8 * d + 8, :CAP], at[d]) <= wants[d]
            at[d] = at[d] + jnp.where(seen, max(step_by, 1), -step_by)
    for d, step in enumerate(steps):
        value = neighbour(step)
        emit(d, windows[d].astype(F32), [lane_gather(value[c], at[d] & 127) for c in range(3)])
    return base


def exchange_kernel(sizes, counts_in, atoms_in, faces_in, places_in, velocity_in, forces_in,
                    own, vel, yblk, slab, zrow, splat, level, level_packed, level_base,
                    counts, atoms, faces, places, velocity, forces, load_sem, drift, half, letter, inbox, zsend,
                    lsend, lrecv, bsend, brecv, ssend, srecv, zs, zr):
    n_gx, n_gy, n_gz = sizes
    me = (lax.axis_index("gx"), lax.axis_index("gy"), lax.axis_index("gz"))

    def at(dx, dy, dz):
        return (
            lax.rem(me[0] + dx + n_gx, n_gx),
            lax.rem(me[1] + dy + n_gy, n_gy),
            lax.rem(me[2] + dz + n_gz, n_gz),
        )

    barrier = pltpu.get_barrier_semaphore()
    around = [
        (dx, dy, dz) for dx in (0, 1) for dy in (-1, 0, 1) for dz in (-1, 0, 1) if (dx, dy, dz) != (0, 0, 0)
    ]
    for step in around:
        pl.semaphore_signal(barrier, inc=1, device_id=at(*step), device_id_type=MESH)

    loads = [
        pltpu.make_async_copy(src, dst, load_sem.at[i])
        for i, (src, dst) in enumerate((
            (places_in, places), (velocity_in, velocity), (forces_in, forces),
            (atoms_in, atoms), (faces_in, faces), (counts_in, counts),
        ))
    ]
    for load in loads:
        load.start()
    for load in loads:
        load.wait()
    for c in range(3):
        for x in range(SX):
            rows = slice(SZ * (SX * c + x), SZ * (SX * c + x) + SZ)
            h = velocity[rows, 0, :] + 0.5 * STEP * forces[rows, 0, :]
            half[c, x] = h
            drift[c, x] = places[rows, 0, :] + STEP * h

    sub8 = iota((8, CAP), 0)
    lane8 = iota((8, CAP), 1)
    lane1 = iota((1, CAP), 1)
    out_letter = jnp.where(sub8 == 6, -1.0, 0.0).astype(F32)
    leaving_cell = jnp.full((1, CAP), -1.0, F32)
    leaving_slot = jnp.full((1, CAP), -1.0, F32)
    for k in range(MIG):
        atom = atoms[0, 0, 0, k]
        face = faces[0, 0, 0, k]
        cell = lax.shift_right_logical(atom, 7)
        slot = atom & 127
        cx = lax.div(cell, SZ)
        cz = lax.rem(cell, SZ)
        axis = lax.shift_right_logical(face, 1)
        up = face & 1
        tile = jnp.zeros((8, CAP), F32)
        for c in range(6):
            source = drift if c < 3 else half
            row = source[c % 3, cx, pl.ds(cz, 1), :]
            tile = jnp.where(sub8 == c, jnp.broadcast_to(row, (8, CAP)), tile)
        column = jnp.sum(jnp.where(lane8 == slot, tile, 0.0), axis=1, keepdims=True)
        sign = (2 * up - 1).astype(F32)
        shift = jnp.where(axis == 2, SIDE[2], SIDE[0]).astype(F32) * sign
        sub_col = iota((8, 1), 0)
        column = column - jnp.where(sub_col == axis, shift, 0.0)
        nx = jnp.where(axis == 0, (1 - up) * (SX - 1), cx)
        nz = jnp.where(axis == 2, (1 - up) * (SZ - 1), cz)
        column = jnp.where(sub_col == 6, (nx * 8 + nz).astype(F32), column)
        out_letter = jnp.where(lane8 == 16 * (face ^ 1) + k, column, out_letter)
        leaving_cell = jnp.where(lane1 == 96 + k, (cx * 8 + cz).astype(F32), leaving_cell)
        leaving_slot = jnp.where(lane1 == 96 + k, slot.astype(F32), leaving_slot)
    letter[...] = out_letter

    pl.semaphore_wait(barrier, len(around))

    posts = []
    for box, step in enumerate(((1, 0, 0), (0, 1, 0), (0, -1, 0), (0, 0, 1), (0, 0, -1))):
        post = pltpu.make_async_remote_copy(
            src_ref=letter, dst_ref=inbox.at[box], send_sem=lsend.at[box], recv_sem=lrecv.at[box],
            device_id=at(*step), device_id_type=MESH,
        )
        post.start()
        posts.append(post)

    count_rows = []
    for x in range(SX):
        row = jnp.zeros((8, CAP), I32)
        for z in range(SZ):
            row = jnp.where(sub8 == z, counts[x, 0, z], row)
        count_rows.append(row)

    for post in posts:
        post.wait_recv()
    got = inbox[4]
    for box, top in ((3, 80), (2, 64), (1, 48), (0, 32)):
        got = jnp.where(lane8 < top, inbox[box], got)
    arriving_cell = jnp.where(lane1 < 96, got[6:7, :], -1.0)
    sub8f = sub8.astype(F32)
    here = []
    gone = []
    for x in range(SX):
        here.append((jnp.broadcast_to(arriving_cell, (8, CAP)) == sub8f + 8.0 * x).astype(F32))
        gone.append((jnp.broadcast_to(leaving_cell, (8, CAP)) == sub8f + 8.0 * x).astype(F32))
    here_all = jnp.concatenate(here, axis=0)
    gone_all = jnp.concatenate(gone, axis=0)
    earlier = (iota((CAP, CAP), 0) < iota((CAP, CAP), 1)).astype(jnp.bfloat16)
    rank = jnp.dot(here_all.astype(jnp.bfloat16), earlier, preferred_element_type=F32)
    slot_table = here_all * (rank + jnp.concatenate(count_rows, axis=0).astype(F32))
    target = jnp.sum(slot_table, axis=0, keepdims=True)
    target = jnp.where(lane1 < 96, target, leaving_slot)
    slot_hit = (jnp.broadcast_to(target, (CAP, CAP)) == iota((CAP, CAP), 0).astype(F32)).astype(jnp.bfloat16)
    pieces = [(here_all - gone_all).astype(jnp.bfloat16)]
    for c in range(6):
        part = here_all * jnp.broadcast_to(jnp.where(lane1 < 96, got[c : c + 1, :], 0.0), here_all.shape)
        for _ in range(3):
            top = part.astype(jnp.bfloat16)
            pieces.append(top)
            part = part - top.astype(F32)
    landed = lax.dot_general(
        jnp.concatenate(pieces, axis=0), slot_hit, (((1,), (1,)), ((), ())), preferred_element_type=F32
    )
    n = SX * 8

    def arrived(c, x):
        base = n * (1 + 3 * c) + 8 * x
        return (
            landed[base : base + SZ] + landed[base + n : base + n + SZ] + landed[base + 2 * n : base + 2 * n + SZ]
        )

    lane6 = iota((SZ, CAP), 1)
    for x in range(SX):
        delta = landed[8 * x : 8 * x + SZ]
        live = (lane6 < count_rows[x][:SZ]).astype(F32) + delta > 0.5
        came = delta > 0.5
        for c in range(3):
            place = jnp.where(came, arrived(c, x), drift[c, x])
            place = jnp.where(live, place, FAR)
            own[c, x, 0:SZ] = place
            own[c, x, SZ:8] = jnp.full((8 - SZ, CAP), FAR, F32)
            zsend[0, c, x : x + 1] = place[0:1]
            zsend[1, c, x : x + 1] = place[SZ - 1 : SZ]
            speed = jnp.where(came, arrived(3 + c, x), half[c, x])
            vel[c, x] = jnp.where(live, speed, 0.0)
    for side in range(2):
        for c in range(3):
            zsend[side, c, SX:8] = jnp.full((8 - SX, CAP), FAR, F32)

    copies = []

    def send(src, dst, ssem, rsem, step):
        copy = pltpu.make_async_remote_copy(
            src_ref=src, dst_ref=dst, send_sem=ssem, recv_sem=rsem, device_id=at(*step), device_id_type=MESH
        )
        copy.start()
        copies.append(copy)

    for dy in (1, -1, 0):
        there = 1 - dy
        for dx in (1, 0):
            for zi, dz in ((0, -1), (1, 1)):
                send(zsend.at[zi], zrow.at[there, dx, 1 - zi], zs.at[there, dx, zi], zr.at[there, dx, 1 - zi], (dx, dy, dz))
    for i, dy in enumerate((1, -1)):
        send(own.at[:, :, 0:SZ], yblk.at[i, :, :, 0:SZ], bsend.at[i], brecv.at[i], (0, dy, 0))
    for dy in (1, -1, 0):
        there = 1 - dy
        for s, x in ((0, 0), (1, SX - 1)):
            send(own.at[:, x, 0:SZ], slab.at[there, s, :, 0:SZ], ssend.at[there, s], srecv.at[there, s], (1, dy, 0))

    def spread(x, _):
        columns = jnp.concatenate([own[c, x] for c in range(3)] + [jnp.zeros((CAP - 24, CAP), F32)], axis=0).T
        for z in range(SZ):
            for c in range(3):
                splat[x, 3 * z + c] = jnp.broadcast_to(columns[:, 8 * c + z : 8 * c + z + 1], (CAP, CAP))
        return 0

    lax.fori_loop(0, SX, spread, 0)

    def arrived_slab(y, side):
        pltpu.make_async_remote_copy(
            src_ref=own.at[:, 0, 0:SZ], dst_ref=slab.at[y, side, :, 0:SZ], send_sem=ssend.at[y, side],
            recv_sem=srecv.at[y, side], device_id=at(1, 0, 0), device_id_type=MESH,
        ).wait_recv()

    def arrived_row(y, g, side):
        pltpu.make_async_remote_copy(
            src_ref=zsend.at[0], dst_ref=zrow.at[y, g, side], send_sem=zs.at[y, g, side],
            recv_sem=zr.at[y, g, side], device_id=at(0, 0, 1), device_id_type=MESH,
        ).wait_recv()

    for side in range(2):
        arrived_slab(1, side)
        for g in range(2):
            arrived_row(1, g, side)

    for c in range(3):
        for xi in range(8):
            if 0 < xi < 7:
                tile = own[c, xi - 1]
                edges = [zrow[1, 0, side, c, xi - 1 : xi] for side in (0, 1)]
            else:
                cell = SX - 1 if xi == 0 else 0
                tile = jnp.concatenate(
                    [slab[1, 1 if xi == 0 else 0, c, 0:SZ], jnp.full((8 - SZ, CAP), FAR, F32)], axis=0
                )
                edges = [zrow[1, 1, side, c, cell : cell + 1] for side in (0, 1)]
            for zi, value in enumerate(three_layers(tile, *edges, c, 0)):
                level[zi, c, xi] = value
    weights = rank_weights()

    def level_rows(p, _):
        for i in range(PER):
            x = PER * p + i

            def neighbour(step):
                value = [level[step[2] + 1, c, x + 1 + step[0]] for c in range(3)]
                if step[0]:
                    value[0] = value[0] + step[0] * SIDE[0]
                return value

            def emit(d, window, chosen):
                level_packed[x, d, 3] = window
                for c in range(3):
                    level_packed[x, d, c] = chosen[c]

            level_base[x] = search(
                LEVEL_STEPS, neighbour, box_of(neighbour((0, 0, 0))), jnp.zeros((8, CAP), F32), weights, emit
            )
        return 0

    lax.fori_loop(0, SX // PER, level_rows, 0)

    for post in posts:
        post.wait_send()
    for copy in copies:
        copy.wait_send()
    for i, dy in enumerate((1, -1)):
        pltpu.make_async_remote_copy(
            src_ref=own.at[:, :, 0:SZ], dst_ref=yblk.at[i, :, :, 0:SZ], send_sem=bsend.at[i], recv_sem=brecv.at[i],
            device_id=at(0, dy, 0), device_id_type=MESH).wait_recv()
    for y in (0, 2):
        for side in range(2):
            arrived_slab(y, side)
            for g in range(2):
                arrived_row(y, g, side)


def force_kernel(own, vel, yblk, slab, zrow, splat, level, level_packed, level_base, out_places, out_velocity, out_forces,
                 near, packed, lists, reduced, sums_of, totals, loops, where_to,
                 places_rows, velocity_rows, forces_rows, store_sem):
    sub8 = iota((8, CAP), 0)
    lane8 = iota((8, CAP), 1)

    for side, y in ((0, 0), (1, 2)):
        for c in range(3):
            for xi in range(8):
                if xi == 0:
                    tile = slab[y, 1, c]
                    edges = [zrow[y, 1, s, c, SX - 1 : SX] for s in (0, 1)]
                elif xi == 7:
                    tile = slab[y, 0, c]
                    edges = [zrow[y, 1, s, c, 0:1] for s in (0, 1)]
                else:
                    tile = yblk[side, c, xi - 1]
                    edges = [zrow[y, 0, s, c, xi - 1 : xi] for s in (0, 1)]
                for zi, value in enumerate(three_layers(tile, *edges, c, y - 1)):
                    near[zi, c, side, xi] = value

    weights = rank_weights()
    stores = ((places_rows, out_places), (velocity_rows, out_velocity), (forces_rows, out_forces))

    def own_cells(x):
        mine = [level[1, c, x + 1] for c in range(3)]
        return mine, mine[0] < 0.5 * FAR

    def build(x, packed):
        mine, live = own_cells(x)

        def neighbour(step):
            dx, dy, dz = step
            value = [near[dz + 1, c, (dy + 1) // 2, x + 1 + dx] for c in range(3)]
            if dx:
                value[0] = value[0] + dx * SIDE[0]
            return value

        for t in range(EAGER):
            for c in range(3):
                lists[x, t, c] = jnp.full((8, CAP), FAR, F32)

        def place(window, chosen):
            for t in range(EAGER):
                for c in range(3):
                    pltpu.store(lists.at[x, t, c], chosen[c], mask=window == float(t))

        def emit(d, window, chosen):
            packed[d, 3] = window
            for c in range(3):
                packed[d, c] = chosen[c]
            place(window, chosen)

        for d in range(len(LEVEL_STEPS)):
            place(level_packed[x, d, 3], [level_packed[x, d, c] for c in range(3)])
        base = search(OTHER_STEPS, neighbour, box_of(mine), level_base[x], weights, emit)
        total = base.astype(I32)
        used = jnp.max(jnp.where(live, lane8 + 1, 0).astype(F32), axis=1, keepdims=True).astype(I32)
        list_steps = lax.shift_right_logical(total + (128 * NL - 1), 7 + (NL - 1))
        row_steps = lax.shift_right_logical(jnp.broadcast_to(used, (8, CAP)) + (8 * ROWS - 1), 3 + {1: 0, 2: 1, 4: 2, 8: 3}[ROWS])
        totals[x, 0] = list_steps
        totals[x, 1] = row_steps
        for kind in range(2):
            for z in range(SZ):
                loops[kind, SZ * x + z] = totals[x, kind, z, 0]
        return functools.reduce(jnp.maximum, [loops[0, SZ * x + z] for z in range(SZ)])

    def build_rows(p, _):
        longest = [build(PER * p + i, packed.at[i]) for i in range(PER)]
        for i in range(PER):

            def fill(t, _):
                tf = t.astype(F32)
                got = [jnp.full((8, CAP), FAR, F32)] * 3
                for source in [level_packed.at[PER * p + i, d] for d in range(len(LEVEL_STEPS))] + [
                    packed.at[i, d] for d in range(len(OTHER_STEPS))
                ]:
                    hit = source[3] == tf
                    got = [jnp.where(hit, source[c], got[c]) for c in range(3)]
                for c in range(3):
                    lists[PER * p + i, t, c] = got[c]
                return 0

            lax.fori_loop(EAGER, longest[i] * NL, fill, 0)
        return 0

    lax.fori_loop(0, SX // PER, build_rows, 0)

    def one_row(x, n_done):
        for z in range(SZ):
            n_list = loops[0, SZ * x + z]
            n_rows = loops[1, SZ * x + z]

            def row_group(g, n_done):
                start = pl.multiple_of(g * GROUP, GROUP)

                def list_step(t, sums):
                    sums = list(sums) if sums else [None] * (3 * ROWS)
                    for u in range(NL):
                        other = [
                            jnp.broadcast_to(lists[x, t * NL + u, c, z : z + 1, :], (8, CAP)) for c in range(3)
                        ]
                        for i in range(ROWS):
                            rows = pl.ds(pl.multiple_of(start + 8 * i, 8), 8)
                            delta = [splat[x, 3 * z + c, rows, :] - other[c] for c in range(3)]
                            square = delta[0] * delta[0] + delta[1] * delta[1] + delta[2] * delta[2]
                            root = lax.rsqrt(jnp.maximum(square, 0.01))
                            second = root * root
                            sixth = second * second * second
                            size = root * ((root * sixth) * (sixth - 0.5) - EDGE / 48.0)
                            size = jnp.where(square < RC * RC, size, 0.0)
                            for c in range(3):
                                term = delta[c] * size
                                sums[3 * i + c] = term if sums[3 * i + c] is None else sums[3 * i + c] + term
                    return tuple(sums)

                sums = lax.fori_loop(1, n_list, list_step, list_step(0, ()))
                for i in range(3 * ROWS):
                    sums_of[n_done, i] = sums[i]
                where_to[0, n_done] = SZ * x + z
                where_to[1, n_done] = g
                return n_done + 1

            n_done = lax.fori_loop(0, n_rows, row_group, n_done)
        return n_done

    n_groups = lax.fori_loop(0, SX, one_row, 0)
    for i in range(BATCH):
        where_to[0, n_groups + i] = SX * SZ
        where_to[1, n_groups + i] = 0

    def sum_lanes(k, _):
        for j in range(BATCH):
            n = k * BATCH + j
            cell = where_to[0, n]
            start = where_to[1, n] * GROUP
            for i in range(ROWS):
                block = jnp.zeros((8, CAP), F32)
                for c in range(3):
                    total = jnp.sum(sums_of[n, 3 * i + c], axis=1, keepdims=True)
                    block = jnp.where(lax.shift_right_logical(lane8, 3) == c, total, block)
                reduced[cell, pl.ds(pl.multiple_of(start + 8 * i, 8), 8), :] = block
        return 0

    lax.fori_loop(0, lax.div(n_groups + (BATCH - 1), BATCH), sum_lanes, 0)

    for x in range(SX):
        mine, live = own_cells(x)
        lane = iota((CAP, CAP), 1) & 7
        columns = reduced[SZ * x]
        for z in range(1, SZ):
            columns = jnp.where(lane == z, reduced[SZ * x + z], columns)
        forces = columns.T
        for c in range(3):
            live6 = live[:SZ]
            force = jnp.where(live6, 48.0 * forces[8 * c : 8 * c + SZ], 0.0)
            rows = pl.ds(SX * SZ * c + SZ * x, SZ)
            forces_rows[rows, 0, :] = force
            velocity_rows[rows, 0, :] = vel[c, x] + 0.5 * STEP * force
            places_rows[rows, 0, :] = jnp.where(live6, mine[c][:SZ], 0.0)
            for i, (src, dst) in enumerate(stores):
                pltpu.make_async_copy(src.at[rows], dst.at[rows], store_sem.at[i]).start()
    for i, (src, dst) in enumerate(stores):
        pltpu.make_async_copy(src, dst, store_sem.at[i]).wait()


def per_device(sizes, places, velocity, forces_old, counts, mig_atom, mig_face):
    shape = places.shape
    flat = (3, SX, SZ, CAP)
    lines = (3 * SX * SZ, 1, CAP)
    anywhere = pl.BlockSpec(memory_space=pltpu.HBM)
    vmem = pl.BlockSpec(memory_space=pltpu.VMEM)
    dma = pltpu.SemaphoreType.DMA
    halo = pl.pallas_call(
        functools.partial(exchange_kernel, sizes),
        out_shape=[
            jax.ShapeDtypeStruct((3, SX, 8, CAP), F32),
            jax.ShapeDtypeStruct(flat, F32),
            jax.ShapeDtypeStruct((2, 3, SX, 8, CAP), F32),
            jax.ShapeDtypeStruct((3, 2, 3, 8, CAP), F32),
            jax.ShapeDtypeStruct((3, 2, 2, 3, 8, CAP), F32),
            jax.ShapeDtypeStruct((SX, 3 * SZ, CAP, CAP), F32),
            jax.ShapeDtypeStruct((3, 3, 8, 8, CAP), F32),
            jax.ShapeDtypeStruct((SX, len(LEVEL_STEPS), 4, 8, CAP), F32),
            jax.ShapeDtypeStruct((SX, 8, CAP), F32),
        ],
        in_specs=[anywhere] * 6,
        out_specs=[vmem] * 9,
        scratch_shapes=[
            pltpu.SMEM(counts.shape, I32),
            pltpu.SMEM(mig_atom.shape, I32),
            pltpu.SMEM(mig_face.shape, I32),
            pltpu.VMEM(lines, F32),
            pltpu.VMEM(lines, F32),
            pltpu.VMEM(lines, F32),
            dma((6,)),
            pltpu.VMEM(flat, F32),
            pltpu.VMEM(flat, F32),
            pltpu.VMEM((8, CAP), F32),
            pltpu.VMEM((5, 8, CAP), F32),
            pltpu.VMEM((2, 3, 8, CAP), F32),
            dma((5,)), dma((5,)), dma((2,)), dma((2,)), dma((3, 2)), dma((3, 2)), dma((3, 2, 2)), dma((3, 2, 2)),
        ],
        compiler_params=pltpu.CompilerParams(collective_id=0, has_side_effects=True, vmem_limit_bytes=8 << 20),
        name="exchange",
    )(*[
        pltpu.with_memory_space_constraint(value, pltpu.HBM)
        for value in (
            counts, mig_atom, mig_face, places.reshape(lines), velocity.reshape(lines), forces_old.reshape(lines)
        )
    ])
    outs = pl.pallas_call(
        force_kernel,
        out_shape=[jax.ShapeDtypeStruct(lines, F32)] * 3,
        in_specs=[vmem] * 9,
        out_specs=[anywhere] * 3,
        scratch_shapes=[
            pltpu.VMEM((3, 3, 2, 8, 8, CAP), F32),
            pltpu.VMEM((PER, len(OTHER_STEPS), 4, 8, CAP), F32),
            pltpu.VMEM((SX, NT, 3, 8, CAP), F32),
            pltpu.VMEM((SX * SZ + 1, CAP, CAP), F32),
            pltpu.VMEM((SX * SZ * (CAP // GROUP) + BATCH, 3 * ROWS, 8, CAP), F32),
            pltpu.VMEM((SX, 2, 8, CAP), I32),
            pltpu.SMEM((2, SX * SZ), I32),
            pltpu.SMEM((2, SX * SZ * (CAP // GROUP) + BATCH), I32),
            pltpu.VMEM(lines, F32),
            pltpu.VMEM(lines, F32),
            pltpu.VMEM(lines, F32),
            dma((3,)),
        ],
        compiler_params=pltpu.CompilerParams(vmem_limit_bytes=24 << 20),
        name="forces",
    )(*halo)
    return tuple(out.reshape(shape) for out in outs)


def solution(mesh):
    sizes = tuple(mesh.shape[a] for a in ("gx", "gy", "gz"))
    block = P(None, "gx", "gy", "gz", None)
    moves = P("gx", "gy", "gz", None)
    return jax.shard_map(
        functools.partial(per_device, sizes),
        mesh=mesh,
        in_specs=(block, block, block, P("gx", "gy", "gz"), moves, moves),
        out_specs=(block, block, block),
        check_vma=False,
    )
```

```python
import functools

import jax
import jax.numpy as jnp
from jax import lax
from jax.experimental import pallas as pl
from jax.experimental.pallas import tpu as pltpu
from jax.sharding import PartitionSpec as P

MESH = pl.DeviceIdType.MESH
F32 = jnp.float32
I32 = jnp.int32
STEP = 0.005
RC = 2.5
SPACING = 1.1
EDGE = 24.0 * (2.0 * RC ** (-13) - RC ** (-7))
SIDE = (4.0 * SPACING, 4.0 * SPACING, SPACING * 8)
FAR = 1.0e4
REACH = RC * 1.0005
SX, SZ, CAP, MIG = 6, 6, 128, 16
ROWS = 4
NL = 2
NT = 32
PER = 3
SPLITS = tuple(range(16, CAP, 16))
EAGER = 4
GROUP = 8 * ROWS
BATCH = 12


def iota(shape, dim):
    return lax.broadcasted_iota(I32, shape, dim)


LANES = lax.GatherDimensionNumbers(
    offset_dims=(), collapsed_slice_dims=(1,), start_index_map=(1,), operand_batching_dims=(0,), start_indices_batching_dims=(0,)
)


def lane_gather(value, index):
    return lax.gather(
        value, index[..., None], LANES, slice_sizes=(1, 1), mode=lax.GatherScatterMode.PROMISE_IN_BOUNDS
    )


STEPS = [(0, 0, 0)] + [
    (dx, dy, dz) for dx in (-1, 0, 1) for dy in (-1, 0, 1) for dz in (-1, 0, 1) if (dx, dy, dz) != (0, 0, 0)
]
LEVEL_STEPS = [step for step in STEPS if step[1] == 0]
OTHER_STEPS = [step for step in STEPS if step[1] != 0]


def three_layers(tile, low, high, c, dy):
    rows = iota((8, CAP), 0)
    below = jnp.where(rows == 0, jnp.broadcast_to(low, (8, CAP)), pltpu.roll(tile, 1, 0))
    above = jnp.where(rows == SZ - 1, jnp.broadcast_to(high, (8, CAP)), pltpu.roll(tile, 7, 0))
    values = [below, tile, above]
    if c == 1 and dy:
        values = [value + dy * SIDE[1] for value in values]
    if c == 2:
        values = [value + dz * SIDE[2] if dz else value for dz, value in zip((-1, 0, 1), values)]
    return values


def box_of(mine):
    live = mine[0] < 0.5 * FAR
    low = [jnp.broadcast_to(jnp.min(mine[c], axis=1, keepdims=True), (8, CAP)) for c in range(3)]
    high = [
        jnp.broadcast_to(jnp.max(jnp.where(live, mine[c], -FAR), axis=1, keepdims=True), (8, CAP)) for c in range(3)
    ]
    return low, high


def rank_weights():
    source, target = iota((CAP, CAP), 0), iota((CAP, CAP), 1)
    return jnp.concatenate(
        [(source <= target).astype(jnp.bfloat16), jnp.ones((CAP, CAP), jnp.bfloat16)]
        + [(source < n).astype(jnp.bfloat16) for n in SPLITS],
        axis=1,
    )


def search(steps, neighbour, box, base, weights, emit):
    lane8 = iota((8, CAP), 1)
    low, high = box
    masks = []
    for step in steps:
        value = neighbour(step)
        gaps = [value[c] - high[c] if s > 0 else low[c] - value[c] for c, s in enumerate(step) if s]
        if len(gaps) > 1:
            gaps = [jnp.maximum(gap, 0.0) for gap in gaps]
            hit = sum(gap * gap for gap in gaps) < REACH * REACH
        elif gaps:
            hit = gaps[0] < REACH
        if not any(s > 0 for s in step):
            alive = value[0] < 0.5 * FAR
            hit = hit & alive if gaps else alive
        masks.append(jnp.where(hit, 1.0, 0.0).astype(F32))
    ranks = jnp.dot(
        jnp.concatenate(masks, axis=0).astype(jnp.bfloat16), weights, preferred_element_type=F32
    )
    wants = []
    windows = []
    at = []
    for d in range(len(steps)):
        rank = [ranks[8 * d : 8 * d + 8, CAP * i : CAP * (i + 1)] for i in range(1, 2 + len(SPLITS))]
        base_int = base.astype(I32)
        want_int = (lane8 - base_int) & 127
        want = want_int.astype(F32)
        wants.append(want)
        windows.append(jnp.where(want < rank[0], lax.shift_right_logical(base_int + want_int, 7), -1))
        base = base + rank[0]
        passed = rank[1:]
        start = jnp.zeros((8, CAP), I32)
        width = CAP
        while passed:
            width //= 2
            half = len(passed) // 2
            over = passed[half] <= want
            start = jnp.where(over, start + width, start) if width < CAP // 2 else jnp.where(over, width, 0)
            passed = [jnp.where(over, b, a) for a, b in zip(passed[:half], passed[half + 1 :])]
        at.append(start + (width // 2 - 1))
    while width > 1:
        width //= 2
        step_by = width // 2
        for d in range(len(steps)):
            seen = lane_gather(ranks[8 * d : 8 * d + 8, :CAP], at[d]) <= wants[d]
            at[d] = at[d] + jnp.where(seen, max(step_by, 1), -step_by)
    for d, step in enumerate(steps):
        value = neighbour(step)
        emit(d, windows[d].astype(F32), [lane_gather(value[c], at[d] & 127) for c in range(3)])
    return base


def exchange_kernel(sizes, counts_in, atoms_in, faces_in, places_in, velocity_in, forces_in,
                    own, vel, yblk, slab, zrow, splat, level, level_packed, level_base,
                    counts, atoms, faces, places, velocity, forces, load_sem, drift, half, letter, inbox, zsend,
                    lsend, lrecv, bsend, brecv, ssend, srecv, zs, zr):
    n_gx, n_gy, n_gz = sizes
    me = (lax.axis_index("gx"), lax.axis_index("gy"), lax.axis_index("gz"))

    def at(dx, dy, dz):
        return (
            lax.rem(me[0] + dx + n_gx, n_gx),
            lax.rem(me[1] + dy + n_gy, n_gy),
            lax.rem(me[2] + dz + n_gz, n_gz),
        )

    barrier = pltpu.get_barrier_semaphore()
    around = [
        (dx, dy, dz) for dx in (0, 1) for dy in (-1, 0, 1) for dz in (-1, 0, 1) if (dx, dy, dz) != (0, 0, 0)
    ]
    for step in around:
        pl.semaphore_signal(barrier, inc=1, device_id=at(*step), device_id_type=MESH)

    loads = [
        pltpu.make_async_copy(src, dst, load_sem.at[i])
        for i, (src, dst) in enumerate((
            (places_in, places), (velocity_in, velocity), (forces_in, forces),
            (atoms_in, atoms), (faces_in, faces), (counts_in, counts),
        ))
    ]
    for load in loads:
        load.start()
    for load in loads:
        load.wait()
    for c in range(3):
        for x in range(SX):
            rows = slice(SZ * (SX * c + x), SZ * (SX * c + x) + SZ)
            h = velocity[rows, 0, :] + 0.5 * STEP * forces[rows, 0, :]
            half[c, x] = h
            drift[c, x] = places[rows, 0, :] + STEP * h

    sub8 = iota((8, CAP), 0)
    lane8 = iota((8, CAP), 1)
    lane1 = iota((1, CAP), 1)
    out_letter = jnp.where(sub8 == 6, -1.0, 0.0).astype(F32)
    leaving_cell = jnp.full((1, CAP), -1.0, F32)
    leaving_slot = jnp.full((1, CAP), -1.0, F32)
    for k in range(MIG):
        atom = atoms[0, 0, 0, k]
        face = faces[0, 0, 0, k]
        cell = lax.shift_right_logical(atom, 7)
        slot = atom & 127
        cx = lax.div(cell, SZ)
        cz = lax.rem(cell, SZ)
        axis = lax.shift_right_logical(face, 1)
        up = face & 1
        tile = jnp.zeros((8, CAP), F32)
        for c in range(6):
            source = drift if c < 3 else half
            row = source[c % 3, cx, pl.ds(cz, 1), :]
            tile = jnp.where(sub8 == c, jnp.broadcast_to(row, (8, CAP)), tile)
        column = jnp.sum(jnp.where(lane8 == slot, tile, 0.0), axis=1, keepdims=True)
        sign = (2 * up - 1).astype(F32)
        shift = jnp.where(axis == 2, SIDE[2], SIDE[0]).astype(F32) * sign
        sub_col = iota((8, 1), 0)
        column = column - jnp.where(sub_col == axis, shift, 0.0)
        nx = jnp.where(axis == 0, (1 - up) * (SX - 1), cx)
        nz = jnp.where(axis == 2, (1 - up) * (SZ - 1), cz)
        column = jnp.where(sub_col == 6, (nx * 8 + nz).astype(F32), column)
        out_letter = jnp.where(lane8 == 16 * (face ^ 1) + k, column, out_letter)
        leaving_cell = jnp.where(lane1 == 96 + k, (cx * 8 + cz).astype(F32), leaving_cell)
        leaving_slot = jnp.where(lane1 == 96 + k, slot.astype(F32), leaving_slot)
    letter[...] = out_letter

    pl.semaphore_wait(barrier, len(around))

    posts = []
    for box, step in enumerate(((1, 0, 0), (0, 1, 0), (0, -1, 0), (0, 0, 1), (0, 0, -1))):
        post = pltpu.make_async_remote_copy(
            src_ref=letter, dst_ref=inbox.at[box], send_sem=lsend.at[box], recv_sem=lrecv.at[box],
            device_id=at(*step), device_id_type=MESH,
        )
        post.start()
        posts.append(post)

    count_rows = []
    for x in range(SX):
        row = jnp.zeros((8, CAP), I32)
        for z in range(SZ):
            row = jnp.where(sub8 == z, counts[x, 0, z], row)
        count_rows.append(row)

    for post in posts:
        post.wait_recv()
    got = inbox[4]
    for box, top in ((3, 80), (2, 64), (1, 48), (0, 32)):
        got = jnp.where(lane8 < top, inbox[box], got)
    arriving_cell = jnp.where(lane1 < 96, got[6:7, :], -1.0)
    sub8f = sub8.astype(F32)
    here = []
    gone = []
    for x in range(SX):
        here.append((jnp.broadcast_to(arriving_cell, (8, CAP)) == sub8f + 8.0 * x).astype(F32))
        gone.append((jnp.broadcast_to(leaving_cell, (8, CAP)) == sub8f + 8.0 * x).astype(F32))
    here_all = jnp.concatenate(here, axis=0)
    gone_all = jnp.concatenate(gone, axis=0)
    earlier = (iota((CAP, CAP), 0) < iota((CAP, CAP), 1)).astype(jnp.bfloat16)
    rank = jnp.dot(here_all.astype(jnp.bfloat16), earlier, preferred_element_type=F32)
    slot_table = here_all * (rank + jnp.concatenate(count_rows, axis=0).astype(F32))
    target = jnp.sum(slot_table, axis=0, keepdims=True)
    target = jnp.where(lane1 < 96, target, leaving_slot)
    slot_hit = (jnp.broadcast_to(target, (CAP, CAP)) == iota((CAP, CAP), 0).astype(F32)).astype(jnp.bfloat16)

    def landing(parts, components):
        for c in components:
            part = here_all * jnp.broadcast_to(jnp.where(lane1 < 96, got[c : c + 1, :], 0.0), here_all.shape)
            for _ in range(3):
                top = part.astype(jnp.bfloat16)
                parts.append(top)
                part = part - top.astype(F32)
        return lax.dot_general(
            jnp.concatenate(parts, axis=0), slot_hit, (((1,), (1,)), ((), ())), preferred_element_type=F32
        )

    landed = landing([(here_all - gone_all).astype(jnp.bfloat16)], range(3))
    n = SX * 8

    def arrived(values, base):
        return (
            values[base : base + SZ] + values[base + n : base + n + SZ] + values[base + 2 * n : base + 2 * n + SZ]
        )

    lane6 = iota((SZ, CAP), 1)
    for x in range(SX):
        delta = landed[8 * x : 8 * x + SZ]
        live = (lane6 < count_rows[x][:SZ]).astype(F32) + delta > 0.5
        came = delta > 0.5
        for c in range(3):
            place = jnp.where(came, arrived(landed, n * (1 + 3 * c) + 8 * x), drift[c, x])
            place = jnp.where(live, place, FAR)
            own[c, x, 0:SZ] = place
            own[c, x, SZ:8] = jnp.full((8 - SZ, CAP), FAR, F32)
            zsend[0, c, x : x + 1] = place[0:1]
            zsend[1, c, x : x + 1] = place[SZ - 1 : SZ]
    for side in range(2):
        for c in range(3):
            zsend[side, c, SX:8] = jnp.full((8 - SX, CAP), FAR, F32)

    copies = []

    def send(src, dst, ssem, rsem, step):
        copy = pltpu.make_async_remote_copy(
            src_ref=src, dst_ref=dst, send_sem=ssem, recv_sem=rsem, device_id=at(*step), device_id_type=MESH
        )
        copy.start()
        copies.append(copy)

    for dy in (1, -1, 0):
        there = 1 - dy
        for dx in (1, 0):
            for zi, dz in ((0, -1), (1, 1)):
                send(zsend.at[zi], zrow.at[there, dx, 1 - zi], zs.at[there, dx, zi], zr.at[there, dx, 1 - zi], (dx, dy, dz))
    for i, dy in enumerate((1, -1)):
        send(own.at[:, :, 0:SZ], yblk.at[i, :, :, 0:SZ], bsend.at[i], brecv.at[i], (0, dy, 0))
    for dy in (1, -1, 0):
        there = 1 - dy
        for s, x in ((0, 0), (1, SX - 1)):
            send(own.at[:, x, 0:SZ], slab.at[there, s, :, 0:SZ], ssend.at[there, s], srecv.at[there, s], (1, dy, 0))

    landed_speed = landing([], range(3, 6))
    for x in range(SX):
        came = landed[8 * x : 8 * x + SZ] > 0.5
        for c in range(3):
            speed = jnp.where(came, arrived(landed_speed, n * 3 * c + 8 * x), half[c, x])
            vel[c, x] = jnp.where(own[c, x, 0:SZ] < 0.5 * FAR, speed, 0.0)

    def spread(x, _):
        columns = jnp.concatenate([own[c, x] for c in range(3)] + [jnp.zeros((CAP - 24, CAP), F32)], axis=0).T
        for z in range(SZ):
            for c in range(3):
                splat[x, 3 * z + c] = jnp.broadcast_to(columns[:, 8 * c + z : 8 * c + z + 1], (CAP, CAP))
        return 0

    lax.fori_loop(0, SX, spread, 0)

    def arrived_slab(y, side):
        pltpu.make_async_remote_copy(
            src_ref=own.at[:, 0, 0:SZ], dst_ref=slab.at[y, side, :, 0:SZ], send_sem=ssend.at[y, side],
            recv_sem=srecv.at[y, side], device_id=at(1, 0, 0), device_id_type=MESH,
        ).wait_recv()

    def arrived_row(y, g, side):
        pltpu.make_async_remote_copy(
            src_ref=zsend.at[0], dst_ref=zrow.at[y, g, side], send_sem=zs.at[y, g, side],
            recv_sem=zr.at[y, g, side], device_id=at(0, 0, 1), device_id_type=MESH,
        ).wait_recv()

    for side in range(2):
        arrived_slab(1, side)
        for g in range(2):
            arrived_row(1, g, side)

    for c in range(3):
        for xi in range(8):
            if 0 < xi < 7:
                tile = own[c, xi - 1]
                edges = [zrow[1, 0, side, c, xi - 1 : xi] for side in (0, 1)]
            else:
                cell = SX - 1 if xi == 0 else 0
                tile = jnp.concatenate(
                    [slab[1, 1 if xi == 0 else 0, c, 0:SZ], jnp.full((8 - SZ, CAP), FAR, F32)], axis=0
                )
                edges = [zrow[1, 1, side, c, cell : cell + 1] for side in (0, 1)]
            for zi, value in enumerate(three_layers(tile, *edges, c, 0)):
                level[zi, c, xi] = value
    weights = rank_weights()

    def level_rows(p, _):
        for i in range(PER):
            x = PER * p + i

            def neighbour(step):
                value = [level[step[2] + 1, c, x + 1 + step[0]] for c in range(3)]
                if step[0]:
                    value[0] = value[0] + step[0] * SIDE[0]
                return value

            def emit(d, window, chosen):
                level_packed[x, d, 3] = window
                for c in range(3):
                    level_packed[x, d, c] = chosen[c]

            level_base[x] = search(
                LEVEL_STEPS, neighbour, box_of(neighbour((0, 0, 0))), jnp.zeros((8, CAP), F32), weights, emit
            )
        return 0

    lax.fori_loop(0, SX // PER, level_rows, 0)

    for post in posts:
        post.wait_send()
    for copy in copies:
        copy.wait_send()
    for i, dy in enumerate((1, -1)):
        pltpu.make_async_remote_copy(
            src_ref=own.at[:, :, 0:SZ], dst_ref=yblk.at[i, :, :, 0:SZ], send_sem=bsend.at[i], recv_sem=brecv.at[i],
            device_id=at(0, dy, 0), device_id_type=MESH).wait_recv()
    for y in (0, 2):
        for side in range(2):
            arrived_slab(y, side)
            for g in range(2):
                arrived_row(y, g, side)


def force_kernel(own, vel, yblk, slab, zrow, splat, level, level_packed, level_base, out_places, out_velocity, out_forces,
                 near, packed, lists, reduced, sums_of, totals, loops, where_to,
                 places_rows, velocity_rows, forces_rows, store_sem):
    sub8 = iota((8, CAP), 0)
    lane8 = iota((8, CAP), 1)

    for side, y in ((0, 0), (1, 2)):
        for c in range(3):
            for xi in range(8):
                if xi == 0:
                    tile = slab[y, 1, c]
                    edges = [zrow[y, 1, s, c, SX - 1 : SX] for s in (0, 1)]
                elif xi == 7:
                    tile = slab[y, 0, c]
                    edges = [zrow[y, 1, s, c, 0:1] for s in (0, 1)]
                else:
                    tile = yblk[side, c, xi - 1]
                    edges = [zrow[y, 0, s, c, xi - 1 : xi] for s in (0, 1)]
                for zi, value in enumerate(three_layers(tile, *edges, c, y - 1)):
                    near[zi, c, side, xi] = value

    weights = rank_weights()
    stores = ((places_rows, out_places), (velocity_rows, out_velocity), (forces_rows, out_forces))

    def own_cells(x):
        mine = [level[1, c, x + 1] for c in range(3)]
        return mine, mine[0] < 0.5 * FAR

    def build(x, packed):
        mine, live = own_cells(x)

        def neighbour(step):
            dx, dy, dz = step
            value = [near[dz + 1, c, (dy + 1) // 2, x + 1 + dx] for c in range(3)]
            if dx:
                value[0] = value[0] + dx * SIDE[0]
            return value

        for t in range(EAGER):
            for c in range(3):
                lists[x, t, c] = jnp.full((8, CAP), FAR, F32)

        def place(window, chosen):
            for t in range(EAGER):
                for c in range(3):
                    pltpu.store(lists.at[x, t, c], chosen[c], mask=window == float(t))

        def emit(d, window, chosen):
            packed[d, 3] = window
            for c in range(3):
                packed[d, c] = chosen[c]
            place(window, chosen)

        for d in range(len(LEVEL_STEPS)):
            place(level_packed[x, d, 3], [level_packed[x, d, c] for c in range(3)])
        base = search(OTHER_STEPS, neighbour, box_of(mine), level_base[x], weights, emit)
        total = base.astype(I32)
        used = jnp.max(jnp.where(live, lane8 + 1, 0).astype(F32), axis=1, keepdims=True).astype(I32)
        list_steps = lax.shift_right_logical(total + (128 * NL - 1), 7 + (NL - 1))
        row_steps = lax.shift_right_logical(jnp.broadcast_to(used, (8, CAP)) + (8 * ROWS - 1), 3 + {1: 0, 2: 1, 4: 2, 8: 3}[ROWS])
        totals[x, 0] = list_steps
        totals[x, 1] = row_steps
        for kind in range(2):
            for z in range(SZ):
                loops[kind, SZ * x + z] = totals[x, kind, z, 0]
        return functools.reduce(jnp.maximum, [loops[0, SZ * x + z] for z in range(SZ)])

    def build_rows(p, _):
        longest = [build(PER * p + i, packed.at[i]) for i in range(PER)]
        for i in range(PER):

            def fill(t, _):
                tf = t.astype(F32)
                got = [jnp.full((8, CAP), FAR, F32)] * 3
                for source in [level_packed.at[PER * p + i, d] for d in range(len(LEVEL_STEPS))] + [
                    packed.at[i, d] for d in range(len(OTHER_STEPS))
                ]:
                    hit = source[3] == tf
                    got = [jnp.where(hit, source[c], got[c]) for c in range(3)]
                for c in range(3):
                    lists[PER * p + i, t, c] = got[c]
                return 0

            lax.fori_loop(EAGER, longest[i] * NL, fill, 0)
        return 0

    lax.fori_loop(0, SX // PER, build_rows, 0)

    def one_row(x, n_done):
        for z in range(SZ):
            n_list = loops[0, SZ * x + z]
            n_rows = loops[1, SZ * x + z]

            def row_group(g, n_done):
                start = pl.multiple_of(g * GROUP, GROUP)

                def list_step(t, sums):
                    sums = list(sums) if sums else [None] * (3 * ROWS)
                    for u in range(NL):
                        other = [
                            jnp.broadcast_to(lists[x, t * NL + u, c, z : z + 1, :], (8, CAP)) for c in range(3)
                        ]
                        for i in range(ROWS):
                            rows = pl.ds(pl.multiple_of(start + 8 * i, 8), 8)
                            delta = [splat[x, 3 * z + c, rows, :] - other[c] for c in range(3)]
                            square = delta[0] * delta[0] + delta[1] * delta[1] + delta[2] * delta[2]
                            root = lax.rsqrt(jnp.maximum(square, 0.01))
                            second = root * root
                            sixth = second * second * second
                            size = root * ((root * sixth) * (sixth - 0.5) - EDGE / 48.0)
                            size = jnp.where(square < RC * RC, size, 0.0)
                            for c in range(3):
                                term = delta[c] * size
                                sums[3 * i + c] = term if sums[3 * i + c] is None else sums[3 * i + c] + term
                    return tuple(sums)

                sums = lax.fori_loop(1, n_list, list_step, list_step(0, ()))
                for i in range(3 * ROWS):
                    sums_of[n_done, i] = sums[i]
                where_to[0, n_done] = SZ * x + z
                where_to[1, n_done] = g
                return n_done + 1

            n_done = lax.fori_loop(0, n_rows, row_group, n_done)
        return n_done

    n_groups = lax.fori_loop(0, SX, one_row, 0)
    for i in range(BATCH):
        where_to[0, n_groups + i] = SX * SZ
        where_to[1, n_groups + i] = 0

    def sum_lanes(k, _):
        for j in range(BATCH):
            n = k * BATCH + j
            cell = where_to[0, n]
            start = where_to[1, n] * GROUP
            for i in range(ROWS):
                block = jnp.zeros((8, CAP), F32)
                for c in range(3):
                    total = jnp.sum(sums_of[n, 3 * i + c], axis=1, keepdims=True)
                    block = jnp.where(lax.shift_right_logical(lane8, 3) == c, total, block)
                reduced[cell, pl.ds(pl.multiple_of(start + 8 * i, 8), 8), :] = block
        return 0

    lax.fori_loop(0, lax.div(n_groups + (BATCH - 1), BATCH), sum_lanes, 0)

    for x in range(SX):
        mine, live = own_cells(x)
        lane = iota((CAP, CAP), 1) & 7
        columns = reduced[SZ * x]
        for z in range(1, SZ):
            columns = jnp.where(lane == z, reduced[SZ * x + z], columns)
        forces = columns.T
        for c in range(3):
            live6 = live[:SZ]
            force = jnp.where(live6, 48.0 * forces[8 * c : 8 * c + SZ], 0.0)
            rows = pl.ds(SX * SZ * c + SZ * x, SZ)
            forces_rows[rows, 0, :] = force
            velocity_rows[rows, 0, :] = vel[c, x] + 0.5 * STEP * force
            places_rows[rows, 0, :] = jnp.where(live6, mine[c][:SZ], 0.0)
            for i, (src, dst) in enumerate(stores):
                pltpu.make_async_copy(src.at[rows], dst.at[rows], store_sem.at[i]).start()
    for i, (src, dst) in enumerate(stores):
        pltpu.make_async_copy(src, dst, store_sem.at[i]).wait()


def per_device(sizes, places, velocity, forces_old, counts, mig_atom, mig_face):
    shape = places.shape
    flat = (3, SX, SZ, CAP)
    lines = (3 * SX * SZ, 1, CAP)
    anywhere = pl.BlockSpec(memory_space=pltpu.HBM)
    vmem = pl.BlockSpec(memory_space=pltpu.VMEM)
    dma = pltpu.SemaphoreType.DMA
    halo = pl.pallas_call(
        functools.partial(exchange_kernel, sizes),
        out_shape=[
            jax.ShapeDtypeStruct((3, SX, 8, CAP), F32),
            jax.ShapeDtypeStruct(flat, F32),
            jax.ShapeDtypeStruct((2, 3, SX, 8, CAP), F32),
            jax.ShapeDtypeStruct((3, 2, 3, 8, CAP), F32),
            jax.ShapeDtypeStruct((3, 2, 2, 3, 8, CAP), F32),
            jax.ShapeDtypeStruct((SX, 3 * SZ, CAP, CAP), F32),
            jax.ShapeDtypeStruct((3, 3, 8, 8, CAP), F32),
            jax.ShapeDtypeStruct((SX, len(LEVEL_STEPS), 4, 8, CAP), F32),
            jax.ShapeDtypeStruct((SX, 8, CAP), F32),
        ],
        in_specs=[anywhere] * 6,
        out_specs=[vmem] * 9,
        scratch_shapes=[
            pltpu.SMEM(counts.shape, I32),
            pltpu.SMEM(mig_atom.shape, I32),
            pltpu.SMEM(mig_face.shape, I32),
            pltpu.VMEM(lines, F32),
            pltpu.VMEM(lines, F32),
            pltpu.VMEM(lines, F32),
            dma((6,)),
            pltpu.VMEM(flat, F32),
            pltpu.VMEM(flat, F32),
            pltpu.VMEM((8, CAP), F32),
            pltpu.VMEM((5, 8, CAP), F32),
            pltpu.VMEM((2, 3, 8, CAP), F32),
            dma((5,)), dma((5,)), dma((2,)), dma((2,)), dma((3, 2)), dma((3, 2)), dma((3, 2, 2)), dma((3, 2, 2)),
        ],
        compiler_params=pltpu.CompilerParams(collective_id=0, has_side_effects=True, vmem_limit_bytes=8 << 20),
        name="exchange",
    )(*[
        pltpu.with_memory_space_constraint(value, pltpu.HBM)
        for value in (
            counts, mig_atom, mig_face, places.reshape(lines), velocity.reshape(lines), forces_old.reshape(lines)
        )
    ])
    outs = pl.pallas_call(
        force_kernel,
        out_shape=[jax.ShapeDtypeStruct(lines, F32)] * 3,
        in_specs=[vmem] * 9,
        out_specs=[anywhere] * 3,
        scratch_shapes=[
            pltpu.VMEM((3, 3, 2, 8, 8, CAP), F32),
            pltpu.VMEM((PER, len(OTHER_STEPS), 4, 8, CAP), F32),
            pltpu.VMEM((SX, NT, 3, 8, CAP), F32),
            pltpu.VMEM((SX * SZ + 1, CAP, CAP), F32),
            pltpu.VMEM((SX * SZ * (CAP // GROUP) + BATCH, 3 * ROWS, 8, CAP), F32),
            pltpu.VMEM((SX, 2, 8, CAP), I32),
            pltpu.SMEM((2, SX * SZ), I32),
            pltpu.SMEM((2, SX * SZ * (CAP // GROUP) + BATCH), I32),
            pltpu.VMEM(lines, F32),
            pltpu.VMEM(lines, F32),
            pltpu.VMEM(lines, F32),
            dma((3,)),
        ],
        compiler_params=pltpu.CompilerParams(vmem_limit_bytes=24 << 20),
        name="forces",
    )(*halo)
    return tuple(out.reshape(shape) for out in outs)


def solution(mesh):
    sizes = tuple(mesh.shape[a] for a in ("gx", "gy", "gz"))
    block = P(None, "gx", "gy", "gz", None)
    moves = P("gx", "gy", "gz", None)
    return jax.shard_map(
        functools.partial(per_device, sizes),
        mesh=mesh,
        in_specs=(block, block, block, P("gx", "gy", "gz"), moves, moves),
        out_specs=(block, block, block),
        check_vma=False,
    )
```
